32 devices in a mesh: ctx: 8 (over y, x, core), tp: 4 (over z).
Axes of the slice: x: 2, y: 2, z: 4, core: 2. Of those that a mesh axis runs over, the one named last changes fastest.
Arguments:
- query_rows: bfloat16 [8192, 4096], P('ctx', 'tp'), may hold values from -6 to 6
- key_rows: bfloat16 [8192, 4096], P('ctx', 'tp'), may hold values from -6 to 6
- value_rows: bfloat16 [8192, 4096], P('ctx', 'tp'), may hold values from -6 to 6
- layer_grad: bfloat16 [8192, 4096], P('ctx', 'tp'), may hold values from -6 to 6
- out_weight: bfloat16 [4096, 4096], P('tp'), may hold values from -0.09375 to 0.09375
Outputs:
- query_grad: bfloat16 [8192, 4096], P('ctx', 'tp')
- key_grad: bfloat16 [8192, 4096], P('ctx', 'tp')
- value_grad: bfloat16 [8192, 4096], P('ctx', 'tp')
The draws below stay inside these ranges and needn't reach their ends.
All inputs are finite; a program needn't handle non-finite values.
Results may differ from the reference program's by a relative error of at most 0.0058.
Values may be sent and summed in bfloat16 or wider, within the bound.
A program may use at most 128 MiB of HBM per device.

```python
import jax
import jax.numpy as jnp
from jax import lax

D = 4096
HEADS = 32
HEAD = 128
TOK_DEV = 1024
TOKENS = 8192
N_CTX = 8


def level_of(key, extent, split, smallest, top_value):
    def one(dim, blocks):
        heights = jax.random.uniform(jax.random.fold_in(jax.random.fold_in(key, 6), dim), (blocks,), jnp.float32, smallest / len(split), top_value / len(split))
        return jnp.repeat(jnp.exp(heights), extent[dim] // blocks).reshape((-1,) + (1,) * (len(extent) - dim - 1))

    gain = one(*split[0])
    for cut in split[1:]:
        gain = gain * one(*cut)
    return gain


def noise(stream_key, shape, spread, most, cuts=(), kind=jnp.bfloat16):
    gain = level_of(stream_key, shape, cuts, -0.22, 0.18) if cuts else 1.0
    result = jax.random.normal(stream_key, shape, jnp.float32) * spread * gain
    return jnp.minimum(jnp.maximum(result, -most), most).astype(kind)


def setup_inputs(seed: int = 0) -> dict:
    splits = jax.random.split(jax.random.key(seed), 6)
    query_rows = noise(splits[0], (TOKENS, HEADS * HEAD), 1.0, 6.0, ((0, 8), (1, 4)))
    key_rows = noise(splits[1], (TOKENS, HEADS * HEAD), 1.0, 6.0, ((0, 8), (1, 4)))
    value_rows = noise(splits[2], (TOKENS, HEADS * HEAD), 1.0, 6.0, ((0, 8), (1, 4)))
    layer_grad = noise(splits[3], (TOKENS, D), 1.0, 6.0, ((0, 8), (1, 4)))
    out_weight = noise(splits[4], (HEADS * HEAD, D), D ** -0.5, 0.09375, ((0, 4),))
    return dict(query_rows=query_rows, key_rows=key_rows, value_rows=value_rows, layer_grad=layer_grad, out_weight=out_weight)


def block_grads(pieces):
    query_blk, key_blk, value_blk, gradient_block, key_value_state, gradient_state = pieces
    factor = (HEAD * TOKENS) ** -0.5
    positions = jnp.arange(TOK_DEV)
    causal = positions[:, None] >= positions[None, :]
    query_float = query_blk.astype(jnp.float32)
    key_float = key_blk.astype(jnp.float32)
    value_float = value_blk.astype(jnp.float32)
    gradient_float = gradient_block.astype(jnp.float32)
    inside_gradient = jnp.einsum("thv,shv->hts", gradient_float, value_float)
    inside_gradient = jnp.where(causal[None], inside_gradient, jnp.float32(0.0)).astype(jnp.bfloat16).astype(jnp.float32)
    inside_query = jnp.einsum("thk,shk->hts", query_float, key_float)
    inside_query = jnp.where(causal[None], inside_query, jnp.float32(0.0)).astype(jnp.bfloat16).astype(jnp.float32)
    key_value_float = key_value_state.astype(jnp.float32)
    gradient_state_float = gradient_state.astype(jnp.float32)
    query_result = jnp.einsum("vmr,rve->mve", inside_gradient, key_float) + jnp.einsum("nde,dze->ndz", gradient_float, key_value_float)
    key_result = jnp.einsum("cxd,xcr->dcr", inside_gradient, query_float) + jnp.einsum("yqr,qmr->yqm", value_float, gradient_state_float)
    value_result = jnp.einsum("kzx,zkm->xkm", inside_query, gradient_float) + jnp.einsum("jaq,aqd->jad", key_float, gradient_state_float)
    return ((factor * query_result).astype(jnp.bfloat16), (factor * key_result).astype(jnp.bfloat16), (factor * value_result).astype(jnp.bfloat16))


def reference(query_rows, key_rows, value_rows, layer_grad, out_weight):
    grad_heads = jnp.dot(layer_grad, out_weight.T, preferred_element_type=jnp.float32).astype(jnp.bfloat16)
    shape4 = (N_CTX, TOK_DEV, HEADS, HEAD)
    query4 = query_rows.reshape(shape4)
    key4 = key_rows.reshape(shape4)
    value4 = value_rows.reshape(shape4)
    grad4 = grad_heads.reshape(shape4)
    key_value_here = jnp.einsum("cthk,cthv->chkv", key4.astype(jnp.float32), value4.astype(jnp.float32))
    gradient_here = jnp.einsum("cthk,cthv->chkv", query4.astype(jnp.float32), grad4.astype(jnp.float32))
    zero_state = jnp.zeros((1, HEADS, HEAD, HEAD), jnp.float32)
    kv_before = jnp.concatenate([zero_state, jnp.cumsum(key_value_here, 0)[:-1]], 0).astype(jnp.bfloat16)
    reversed_sum = jnp.cumsum(gradient_here[::-1], 0)[::-1]
    grad_after = jnp.concatenate([reversed_sum[1:], zero_state], 0).astype(jnp.bfloat16)
    query_result, key_result, value_result = lax.map(block_grads, (query4, key4, value4, grad4, kv_before, grad_after))
    flat = (TOKENS, HEADS * HEAD)
    return (query_result.reshape(flat), key_result.reshape(flat), value_result.reshape(flat))
```

```python
import functools

import jax
import jax.numpy as jnp
from jax import lax
from jax.experimental import pallas as pl
from jax.experimental.pallas import tpu as pltpu
from jax.sharding import PartitionSpec as P

HEAD = 128
MESH = pl.DeviceIdType.MESH
F32 = jnp.float32
BF16 = jnp.bfloat16
NT = (((1,), (1,)), ((), ()))
NN = (((1,), (0,)), ((), ()))
TN = (((0,), (0,)), ((), ()))


def mm(a, b, dims):
    return lax.dot_general(a, b, dims, preferred_element_type=F32)


def attention_head(read, state_kv, state_grad, write, tokens, size, factor):
    count = tokens // size
    pieces = [read(i) for i in range(count)]
    rows = lax.broadcasted_iota(jnp.int32, (size, size), 0)
    cols = lax.broadcasted_iota(jnp.int32, (size, size), 1)
    causal = rows >= cols
    after = [None] * count
    total = state_grad
    for i in reversed(range(count)):
        after[i] = total.astype(BF16)
        if i:
            q, _, _, g = pieces[i]
            total = total + mm(q, g, TN)
    before = state_kv
    for i in range(count):
        q, k, v, g = pieces[i]
        inner_grad = jnp.where(causal, mm(g, v, NT), 0.0).astype(BF16)
        inner_query = jnp.where(causal, mm(q, k, NT), 0.0).astype(BF16)
        query = mm(inner_grad, k, NN) + mm(g, before.astype(BF16), NT)
        key = mm(inner_grad, q, TN) + mm(v, after[i], NT)
        value = mm(inner_query, g, TN) + mm(k, after[i], NN)
        write(i, (factor * query).astype(BF16), (factor * key).astype(BF16), (factor * value).astype(BF16))
        if i < count - 1:
            before = before + mm(k, v, TN)


def attention_kernel(size, factor, q_ref, k_ref, v_ref, g_ref, kv_ref, grad_ref, qo_ref, ko_ref, vo_ref):
    tokens = q_ref.shape[0]

    def read(i):
        at = pl.ds(i * size, size)
        return q_ref[at, :], k_ref[at, :], v_ref[at, :], g_ref[at, :]

    def write(i, query, key, value):
        at = pl.ds(i * size, size)
        qo_ref[at, :] = query
        ko_ref[at, :] = key
        vo_ref[at, :] = value

    attention_head(read, kv_ref[0].astype(F32), grad_ref[0].astype(F32), write, tokens, size, factor)


def attention(q, k, v, g, kv_before, grad_after, factor):
    tokens, columns = q.shape
    size = min(256, tokens)
    rows = pl.BlockSpec((tokens, HEAD), lambda h: (0, h))
    state = pl.BlockSpec((1, HEAD, HEAD), lambda h: (h, 0, 0))
    return pl.pallas_call(
        functools.partial(attention_kernel, size, factor),
        grid=(columns // HEAD,),
        out_shape=[jax.ShapeDtypeStruct(q.shape, BF16)] * 3,
        in_specs=[rows] * 4 + [state] * 2,
        out_specs=[rows] * 3,
    )(q, k, v, g, kv_before, grad_after)


def gather_kernel(
    n_ctx, q_hbm, k_hbm, v_hbm, lg_hbm, w_hbm, g_ref, kv_ref, grad_ref,
    q_buf, k_buf, v_buf, lg, w, far, part_out, part_in,
    kv_out, kv_in, grad_out, grad_in,
    load_sem, ends_sem, mids_sem, lg_recv, fwd_sem, part_sem, part_recv,
    far_sem, far_recv, twin_sem, twin_recv, kv_sem, kv_recv, grad_sem, grad_recv,
):
    me = lax.axis_index("ctx")
    z = lax.axis_index("tp")
    tokens, width = lg_hbm.shape
    columns = w_hbm.shape[0]
    heads = columns // HEAD
    chunks = lg_recv.shape[1]
    size = tokens // chunks
    pieces = far_sem.shape[0]
    half = columns // 2
    piece = half // pieces
    twin = me + 1 - 2 * (me % 2)
    core = me % 2
    is_end = (z == 0) | (z == 3)
    is_mid = (z == 1) | (z == 2)
    low = z // 2
    end = 3 * low
    mid = 1 + low
    mid2 = 2 - low
    end2 = 3 - end
    far_col = pl.multiple_of((1 - low) * 2 * width, 2 * width)
    near_col = pl.multiple_of(low * 2 * width, 2 * width)

    def col(part):
        return pl.ds(pl.multiple_of(part * width, width), width)

    def row(i):
        return pl.ds(pl.multiple_of(i * size, size), size)

    barrier = pltpu.get_barrier_semaphore()
    for d in range(1, n_ctx):
        pl.semaphore_signal(barrier, inc=1, device_id=((me + d) % n_ctx, z), device_id_type=MESH)

    @pl.when(is_end)
    def _():
        pl.semaphore_signal(barrier, inc=1, device_id=(me, mid), device_id_type=MESH)
        pl.semaphore_wait(barrier, n_ctx)

    @pl.when(is_mid)
    def _():
        pl.semaphore_signal(barrier, inc=1, device_id=(me, end), device_id_type=MESH)
        pl.semaphore_signal(barrier, inc=1, device_id=(me, mid2), device_id_type=MESH)
        pl.semaphore_wait(barrier, n_ctx + 1)

    def remote(src, dst, send, recv, target):
        return pltpu.make_async_remote_copy(
            src_ref=src, dst_ref=dst, send_sem=send, recv_sem=recv, device_id=target, device_id_type=MESH)

    def lg_from_hbm(i, sems, target_z):
        return remote(lg_hbm.at[row(i), :], lg.at[row(i), col(z)], sems.at[i], lg_recv.at[z, i], (me, target_z))

    def lg_forward(i):
        place = lg.at[row(i), col(end)]
        return remote(place, place, fwd_sem.at[i], lg_recv.at[end, i], (me, mid2))

    def lg_arrival(part, i):
        place = lg.at[row(i), col(part)]
        return remote(place, place, fwd_sem.at[i], lg_recv.at[part, i], (me, mid2))

    def far_rows(which, p):
        return pl.ds(pl.multiple_of(which * half + p * piece, piece), piece)

    def far_send(p):
        return remote(w_hbm.at[far_rows(core, p), pl.ds(far_col, 2 * width)], far.at[far_rows(core, p), :],
                      far_sem.at[p], far_recv.at[p], (me, mid))

    def far_share(p):
        place = far.at[far_rows(core, p), :]
        return remote(place, place, twin_sem.at[p], twin_recv.at[p], (twin, z))

    def far_twin(p):
        place = far.at[far_rows(1 - core, p), :]
        return remote(place, place, twin_sem.at[p], twin_recv.at[p], (twin, z))

    def part_send(i):
        return remote(part_out.at[row(i), :], part_in.at[row(i), :], part_sem.at[i], part_recv.at[i], (me, end))

    @pl.when(is_end)
    def _():
        for p in range(pieces):
            far_send(p).start()

        @pl.loop(0, chunks)
        def _(i):
            lg_from_hbm(i, ends_sem, mid).start()

    @pl.when(is_mid)
    def _():
        @pl.loop(0, chunks)
        def _(i):
            lg_from_hbm(i, ends_sem, end).start()
            lg_from_hbm(i, mids_sem, mid2).start()

    loads = [
        pltpu.make_async_copy(k_hbm, k_buf, load_sem.at[0]),
        pltpu.make_async_copy(v_hbm, v_buf, load_sem.at[1]),
        pltpu.make_async_copy(q_hbm, q_buf, load_sem.at[2]),
        pltpu.make_async_copy(lg_hbm, lg.at[:, col(z)], load_sem.at[3]),
        pltpu.make_async_copy(w_hbm, w, load_sem.at[4]),
    ]
    for load in loads:
        load.start()
    loads[0].wait()
    loads[1].wait()

    def head(h):
        return pl.ds(pl.multiple_of(h * HEAD, HEAD), HEAD)

    @pl.loop(0, heads)
    def _(h):
        kv_out[h] = mm(k_buf[:, head(h)], v_buf[:, head(h)], TN).astype(BF16)

    for d in range(1, n_ctx):
        @pl.when(me + d < n_ctx)
        def _():
            remote(kv_out, kv_in.at[d - 1], kv_sem.at[d - 1], kv_recv.at[d - 1], ((me + d) % n_ctx, z)).start()
    for load in loads[2:]:
        load.wait()

    tile = min(256, columns)

    @pl.when(is_end)
    def _():
        @pl.loop(0, chunks)
        def _(i):
            lg_arrival(mid, i).wait_recv()
            part_send(i).wait_recv()

            @pl.loop(0, columns // tile)
            def _(n):
                out = pl.ds(pl.multiple_of(n * tile, tile), tile)
                near = pl.ds(near_col, 2 * width)
                total = mm(lg[row(i), near], w[out, near], NT)
                g_ref[row(i), out] = (total + part_in[row(i), out].astype(F32)).astype(BF16)

    @pl.when(is_mid)
    def _():
        for p in range(pieces):
            far_send(p).wait_recv()
            far_share(p).start()
        lg_arrival(end, 0).wait_recv()
        lg_forward(0).start()
        for p in range(pieces):
            far_twin(p).wait_recv()

        @pl.loop(0, chunks)
        def _(i):
            @pl.when(i < chunks - 1)
            def _():
                lg_arrival(end, i + 1).wait_recv()
                lg_forward(i + 1).start()

            lg_arrival(mid2, i).wait_recv()
            lg_arrival(end2, i).wait_recv()

            @pl.loop(0, columns // tile)
            def _(n):
                out = pl.ds(pl.multiple_of(n * tile, tile), tile)
                part_out[row(i), out] = mm(lg[row(i), pl.ds(far_col, 2 * width)], far[out, :], NT).astype(BF16)

            part_send(i).start()

            @pl.loop(0, columns // tile)
            def _(n):
                out = pl.ds(pl.multiple_of(n * tile, tile), tile)
                g_ref[row(i), out] = mm(lg[row(i), :], w[out, :], NT).astype(BF16)

    @pl.loop(0, heads)
    def _(h):
        grad_out[h] = mm(q_buf[:, head(h)], g_ref[:, head(h)], TN).astype(BF16)

    for d in range(1, n_ctx):
        @pl.when(me >= d)
        def _():
            remote(grad_out, grad_in.at[d - 1], grad_sem.at[d - 1], grad_recv.at[d - 1], ((me + n_ctx - d) % n_ctx, z)).start()

    def add_up(source, recv, send, target, out_ref, wanted):
        for d in range(1, n_ctx):
            @pl.when(wanted(d))
            def _(d=d):
                remote(source.at[d - 1], source.at[d - 1], send.at[d - 1], recv.at[d - 1], (target, z)).wait_recv()

            @pl.when(jnp.logical_not(wanted(d)))
            def _(d=d):
                source[d - 1] = jnp.zeros(source.shape[1:], BF16)

        @pl.loop(0, heads)
        def _(h):
            total = source[0, h].astype(F32)
            for d in range(2, n_ctx):
                total = total + source[d - 1, h].astype(F32)
            out_ref[h] = total.astype(BF16)

    add_up(kv_in, kv_recv, kv_sem, twin, kv_ref, lambda d: me >= d)
    add_up(grad_in, grad_recv, grad_sem, twin, grad_ref, lambda d: me + d < n_ctx)

    for d in range(1, n_ctx):
        @pl.when(me + d < n_ctx)
        def _():
            remote(kv_out, kv_in.at[d - 1], kv_sem.at[d - 1], kv_recv.at[d - 1], (twin, z)).wait_send()

        @pl.when(me >= d)
        def _():
            remote(grad_out, grad_in.at[d - 1], grad_sem.at[d - 1], grad_recv.at[d - 1], (twin, z)).wait_send()

    @pl.when(is_end)
    def _():
        for p in range(pieces):
            far_send(p).wait_send()

        @pl.loop(0, chunks)
        def _(i):
            lg_from_hbm(i, ends_sem, mid).wait_send()

    @pl.when(is_mid)
    def _():
        for p in range(pieces):
            far_share(p).wait_send()

        @pl.loop(0, chunks)
        def _(i):
            lg_from_hbm(i, ends_sem, end).wait_send()
            lg_from_hbm(i, mids_sem, mid2).wait_send()
            lg_forward(i).wait_send()
            part_send(i).wait_send()


def gather(q, k, v, lg, w, n_ctx):
    tokens, width = lg.shape
    columns = w.shape[0]
    heads = columns // HEAD
    chunks = 8 if tokens % 128 == 0 and tokens >= 1024 else 1
    pieces = 4
    dma = pltpu.SemaphoreType.DMA
    state = (heads, HEAD, HEAD)
    slots = (n_ctx - 1,) + state
    any_spec = pl.BlockSpec(memory_space=pl.ANY)
    vmem_spec = pl.BlockSpec(memory_space=pltpu.VMEM)
    return pl.pallas_call(
        functools.partial(gather_kernel, n_ctx),
        out_shape=[
            jax.ShapeDtypeStruct((tokens, columns), BF16),
            jax.ShapeDtypeStruct(state, BF16),
            jax.ShapeDtypeStruct(state, BF16),
        ],
        in_specs=[any_spec] * 5,
        out_specs=[vmem_spec] * 3,
        scratch_shapes=[
            pltpu.VMEM((tokens, columns), BF16),
            pltpu.VMEM((tokens, columns), BF16),
            pltpu.VMEM((tokens, columns), BF16),
            pltpu.VMEM((tokens, 4 * width), BF16),
            pltpu.VMEM(w.shape, BF16),
            pltpu.VMEM((columns, 2 * width), BF16),
            pltpu.VMEM((tokens, columns), BF16),
            pltpu.VMEM((tokens, columns), BF16),
            pltpu.VMEM(state, BF16),
            pltpu.VMEM(slots, BF16),
            pltpu.VMEM(state, BF16),
            pltpu.VMEM(slots, BF16),
            dma((5,)), dma((chunks,)), dma((chunks,)), dma((4, chunks)), dma((chunks,)),
            dma((chunks,)), dma((chunks,)),
            dma((pieces,)), dma((pieces,)), dma((pieces,)), dma((pieces,)),
            dma((n_ctx - 1,)), dma((n_ctx - 1,)), dma((n_ctx - 1,)), dma((n_ctx - 1,)),
        ],
        compiler_params=pltpu.CompilerParams(
            collective_id=0, has_side_effects=True, vmem_limit_bytes=60 * 1024 * 1024),
    )(q, k, v, lg, w)


def gather_plain(q, k, v, lg, w):
    tokens, columns = q.shape
    heads = columns // HEAD
    me = lax.axis_index("ctx")
    g = lax.dot_general(lax.all_gather(lg, "tp", axis=1, tiled=True), w, NT, preferred_element_type=F32).astype(BF16)
    three = (tokens, heads, HEAD)
    kv_here = jnp.einsum("lbg,lbz->bgz", k.reshape(three), v.reshape(three), preferred_element_type=F32)
    grad_here = jnp.einsum("lbg,lbz->bgz", q.reshape(three), g.reshape(three), preferred_element_type=F32)

    def pick(mine, lower):
        stacked = lax.all_gather(mine[None], "ctx", axis=0, tiled=True)
        index = jnp.arange(stacked.shape[0])
        chosen = index < me if lower else index > me
        return jnp.sum(jnp.where(chosen[:, None, None, None], stacked, 0.0), 0).astype(BF16)

    return g, pick(kv_here, True), pick(grad_here, False)


def local(q, k, v, lg, w):
    n_ctx = lax.axis_size("ctx")
    n_tp = lax.axis_size("tp")
    factor = float((HEAD * q.shape[0] * n_ctx) ** (-0.5))
    if n_tp == 4 and n_ctx % 2 == 0:
        g, kv_before, grad_after = gather(q, k, v, lg, w, n_ctx)
    else:
        g, kv_before, grad_after = gather_plain(q, k, v, lg, w)
    return tuple(attention(q, k, v, g, kv_before, grad_after, factor))


def solution(mesh):
    return jax.shard_map(
        local,
        mesh=mesh,
        in_specs=(P("ctx", "tp"), P("ctx", "tp"), P("ctx", "tp"), P("ctx", "tp"), P("tp", None)),
        out_specs=(P("ctx", "tp"), P("ctx", "tp"), P("ctx", "tp")),
        check_vma=False,
    )
```

```python
import functools

import jax
import jax.numpy as jnp
from jax import lax
from jax.experimental import pallas as pl
from jax.experimental.pallas import tpu as pltpu
from jax.sharding import PartitionSpec as P

HEAD = 128
MESH = pl.DeviceIdType.MESH
F32 = jnp.float32
BF16 = jnp.bfloat16
NT = (((1,), (1,)), ((), ()))
NN = (((1,), (0,)), ((), ()))
TN = (((0,), (0,)), ((), ()))


def mm(a, b, dims):
    return lax.dot_general(a, b, dims, preferred_element_type=F32)


def attention_head(read, state_kv, state_grad, write, tokens, size, factor):
    count = tokens // size
    pieces = [read(i) for i in range(count)]
    rows = lax.broadcasted_iota(jnp.int32, (size, size), 0)
    cols = lax.broadcasted_iota(jnp.int32, (size, size), 1)
    causal = rows >= cols
    after = [None] * count
    total = state_grad
    for i in reversed(range(count)):
        after[i] = total.astype(BF16)
        if i:
            q, _, _, g = pieces[i]
            total = total + mm(q, g, TN)
    before = state_kv
    for i in range(count):
        q, k, v, g = pieces[i]
        inner_grad = jnp.where(causal, mm(g, v, NT), 0.0).astype(BF16)
        inner_query = jnp.where(causal, mm(q, k, NT), 0.0).astype(BF16)
        query = mm(inner_grad, k, NN) + mm(g, before.astype(BF16), NT)
        key = mm(inner_grad, q, TN) + mm(v, after[i], NT)
        value = mm(inner_query, g, TN) + mm(k, after[i], NN)
        write(i, (factor * query).astype(BF16), (factor * key).astype(BF16), (factor * value).astype(BF16))
        if i < count - 1:
            before = before + mm(k, v, TN)


def attention_kernel(size, factor, q_ref, k_ref, v_ref, g_ref, kv_ref, grad_ref, qo_ref, ko_ref, vo_ref):
    tokens = q_ref.shape[0]

    def read(i):
        at = pl.ds(i * size, size)
        return q_ref[at, :], k_ref[at, :], v_ref[at, :], g_ref[at, :]

    def write(i, query, key, value):
        at = pl.ds(i * size, size)
        qo_ref[at, :] = query
        ko_ref[at, :] = key
        vo_ref[at, :] = value

    attention_head(read, kv_ref[0].astype(F32), grad_ref[0].astype(F32), write, tokens, size, factor)


def attention(q, k, v, g, kv_before, grad_after, factor):
    tokens, columns = q.shape
    size = min(256, tokens)
    rows = pl.BlockSpec((tokens, HEAD), lambda h: (0, h))
    state = pl.BlockSpec((1, HEAD, HEAD), lambda h: (h, 0, 0))
    return pl.pallas_call(
        functools.partial(attention_kernel, size, factor),
        grid=(columns // HEAD,),
        out_shape=[jax.ShapeDtypeStruct(q.shape, BF16)] * 3,
        in_specs=[rows] * 4 + [state] * 2,
        out_specs=[rows] * 3,
    )(q, k, v, g, kv_before, grad_after)


def gather_kernel(
    n_ctx, factor, q_hbm, k_hbm, v_hbm, lg_hbm, w_hbm, qo_hbm, ko_hbm, vo_hbm,
    q_buf, k_buf, v_buf, g_ref, lg, w, far, part_out, part_in,
    qo_buf, ko_buf, vo_buf, key_part, value_part, kv_sums, kv_state, grad_sums, after,
    kv_out, kv_in, grad_out, grad_twin, pair, pair_in, rest, rest_in,
    load_sem, ends_sem, mids_sem, lg_recv, fwd_sem, part_sem, part_recv,
    far_sem, far_recv, twin_sem, twin_recv, kv_sem, kv_recv, pair_sem, pair_recv, core_sem, core_recv, out_sem,
):
    me = lax.axis_index("ctx")
    z = lax.axis_index("tp")
    tokens, width = lg_hbm.shape
    columns = w_hbm.shape[0]
    heads = columns // HEAD
    chunks = lg_recv.shape[1]
    size = tokens // chunks
    pieces = far_sem.shape[0]
    half = columns // 2
    piece = half // pieces
    twin = me + 1 - 2 * (me % 2)
    core = me % 2
    is_end = (z == 0) | (z == 3)
    is_mid = (z == 1) | (z == 2)
    low = z // 2
    end = 3 * low
    mid = 1 + low
    mid2 = 2 - low
    end2 = 3 - end
    far_col = pl.multiple_of((1 - low) * 2 * width, 2 * width)
    near_col = pl.multiple_of(low * 2 * width, 2 * width)

    def col(part):
        return pl.ds(pl.multiple_of(part * width, width), width)

    def row(i):
        return pl.ds(pl.multiple_of(i * size, size), size)

    barrier = pltpu.get_barrier_semaphore()
    for d in range(1, n_ctx):
        pl.semaphore_signal(barrier, inc=1, device_id=((me + d) % n_ctx, z), device_id_type=MESH)

    @pl.when(is_end)
    def _():
        pl.semaphore_signal(barrier, inc=1, device_id=(me, mid), device_id_type=MESH)
        pl.semaphore_wait(barrier, n_ctx)

    @pl.when(is_mid)
    def _():
        pl.semaphore_signal(barrier, inc=1, device_id=(me, end), device_id_type=MESH)
        pl.semaphore_signal(barrier, inc=1, device_id=(me, mid2), device_id_type=MESH)
        pl.semaphore_wait(barrier, n_ctx + 1)

    def remote(src, dst, send, recv, target):
        return pltpu.make_async_remote_copy(
            src_ref=src, dst_ref=dst, send_sem=send, recv_sem=recv, device_id=target, device_id_type=MESH)

    def lg_from_hbm(i, sems, target_z):
        return remote(lg_hbm.at[row(i), :], lg.at[row(i), col(z)], sems.at[i], lg_recv.at[z, i], (me, target_z))

    def lg_forward(i):
        place = lg.at[row(i), col(end)]
        return remote(place, place, fwd_sem.at[i], lg_recv.at[end, i], (me, mid2))

    def lg_arrival(part, i):
        place = lg.at[row(i), col(part)]
        return remote(place, place, fwd_sem.at[i], lg_recv.at[part, i], (me, mid2))

    def far_rows(which, p):
        return pl.ds(pl.multiple_of(which * half + p * piece, piece), piece)

    def far_send(p):
        return remote(w_hbm.at[far_rows(core, p), pl.ds(far_col, 2 * width)], far.at[far_rows(core, p), :],
                      far_sem.at[p], far_recv.at[p], (me, mid))

    def far_share(p):
        place = far.at[far_rows(core, p), :]
        return remote(place, place, twin_sem.at[p], twin_recv.at[p], (twin, z))

    def far_twin(p):
        place = far.at[far_rows(1 - core, p), :]
        return remote(place, place, twin_sem.at[p], twin_recv.at[p], (twin, z))

    def part_send(i):
        return remote(part_out.at[row(i), :], part_in.at[row(i), :], part_sem.at[i], part_recv.at[i], (me, end))

    @pl.when(is_end)
    def _():
        for p in range(pieces):
            far_send(p).start()

        @pl.loop(0, chunks)
        def _(i):
            lg_from_hbm(i, ends_sem, mid).start()

    @pl.when(is_mid)
    def _():
        @pl.loop(0, chunks)
        def _(i):
            lg_from_hbm(i, ends_sem, end).start()
            lg_from_hbm(i, mids_sem, mid2).start()

    loads = [
        pltpu.make_async_copy(k_hbm, k_buf, load_sem.at[0]),
        pltpu.make_async_copy(v_hbm, v_buf, load_sem.at[1]),
        pltpu.make_async_copy(q_hbm, q_buf, load_sem.at[2]),
        pltpu.make_async_copy(lg_hbm, lg.at[:, col(z)], load_sem.at[3]),
        pltpu.make_async_copy(w_hbm, w, load_sem.at[4]),
    ]
    for load in loads:
        load.start()
    loads[0].wait()
    loads[1].wait()

    def head(h):
        return pl.ds(pl.multiple_of(h * HEAD, HEAD), HEAD)

    blocks = kv_sums.shape[0]
    block = tokens // blocks
    per = chunks // blocks
    half_heads = heads // 2
    rows_at = lax.broadcasted_iota(jnp.int32, (block, block), 0)
    cols_at = lax.broadcasted_iota(jnp.int32, (block, block), 1)
    causal = rows_at >= cols_at

    def span(c):
        return pl.ds(pl.multiple_of(c * block, block), block)

    @pl.loop(0, heads)
    def _(h):
        total = jnp.zeros((HEAD, HEAD), F32)
        for c in range(blocks):
            here = mm(k_buf[span(c), head(h)], v_buf[span(c), head(h)], TN)
            kv_sums[c, h] = here
            total = total + here
        kv_out[h] = total.astype(BF16)

    for d in range(1, n_ctx):
        @pl.when(me + d < n_ctx)
        def _():
            remote(kv_out, kv_in.at[d - 1], kv_sem.at[d - 1], kv_recv.at[d - 1], ((me + d) % n_ctx, z)).start()
    for load in loads[2:]:
        load.wait()

    tile = min(256, columns)

    def finish_kv():
        for d in range(1, n_ctx):
            @pl.when(me >= d)
            def _():
                remote(kv_in.at[d - 1], kv_in.at[d - 1], kv_sem.at[d - 1], kv_recv.at[d - 1], (twin, z)).wait_recv()

            @pl.when(me < d)
            def _():
                kv_in[d - 1] = jnp.zeros(kv_in.shape[1:], BF16)

        @pl.loop(0, heads)
        def _(h):
            total = kv_in[0, h].astype(F32)
            for d in range(2, n_ctx):
                total = total + kv_in[d - 1, h].astype(F32)
            for c in range(blocks):
                kv_state[c, h] = total.astype(BF16)
                total = total + kv_sums[c, h]

    def attend(c, h):
        at, hd = span(c), head(h)
        q, k, v, g = q_buf[at, hd], k_buf[at, hd], v_buf[at, hd], g_ref[at, hd]
        inner_grad = jnp.where(causal, mm(g, v, NT), 0.0).astype(BF16)
        inner_query = jnp.where(causal, mm(q, k, NT), 0.0).astype(BF16)
        query = mm(inner_grad, k, NN) + mm(g, kv_state[c, h], NT)
        qo_buf[at, hd] = (factor * query).astype(BF16)
        key_part[at, hd] = mm(inner_grad, q, TN)
        value_part[at, hd] = mm(inner_query, g, TN)

    def attend_step(i):
        @pl.when(i >= per)
        def _():
            share = heads // per

            @pl.loop(0, share)
            def _(j):
                attend(i // per - 1, (i % per) * share + j)

        @pl.when(i % per == per - 1)
        def _():
            @pl.loop(0, heads)
            def _(h):
                c = i // per
                grad_sums[c, h] = mm(q_buf[span(c), head(h)], g_ref[span(c), head(h)], TN)

    @pl.when(is_end)
    def _():
        finish_kv()

        @pl.loop(0, chunks)
        def _(i):
            lg_arrival(mid, i).wait_recv()
            part_send(i).wait_recv()

            @pl.loop(0, columns // tile)
            def _(n):
                out = pl.ds(pl.multiple_of(n * tile, tile), tile)
                near = pl.ds(near_col, 2 * width)
                total = mm(lg[row(i), near], w[out, near], NT)
                g_ref[row(i), out] = (total + part_in[row(i), out].astype(F32)).astype(BF16)

            attend_step(i)

    @pl.when(is_mid)
    def _():
        for p in range(pieces):
            far_send(p).wait_recv()
            far_share(p).start()
        finish_kv()
        lg_arrival(end, 0).wait_recv()
        lg_forward(0).start()
        for p in range(pieces):
            far_twin(p).wait_recv()

        @pl.loop(0, chunks)
        def _(i):
            @pl.when(i < chunks - 1)
            def _():
                lg_arrival(end, i + 1).wait_recv()
                lg_forward(i + 1).start()

            lg_arrival(mid2, i).wait_recv()
            lg_arrival(end2, i).wait_recv()

            @pl.loop(0, columns // tile)
            def _(n):
                out = pl.ds(pl.multiple_of(n * tile, tile), tile)
                part_out[row(i), out] = mm(lg[row(i), pl.ds(far_col, 2 * width)], far[out, :], NT).astype(BF16)

            part_send(i).start()

            @pl.loop(0, columns // tile)
            def _(n):
                out = pl.ds(pl.multiple_of(n * tile, tile), tile)
                g_ref[row(i), out] = mm(lg[row(i), :], w[out, :], NT).astype(BF16)

            attend_step(i)

    chip = me // 2
    n_chips = n_ctx // 2
    mine = pl.ds(pl.multiple_of(core * half_heads, half_heads), half_heads)
    other = pl.ds(pl.multiple_of((1 - core) * half_heads, half_heads), half_heads)

    @pl.loop(0, heads)
    def _(h):
        total = grad_sums[0, h]
        for c in range(1, blocks):
            total = total + grad_sums[c, h]
        after[h] = total
        grad_out[h] = total.astype(BF16)

    swap = remote(grad_out.at[other], grad_twin.at[other], core_sem.at[0], core_recv.at[0], (twin, z))
    swap_in = remote(grad_out.at[mine], grad_twin.at[mine], core_sem.at[0], core_recv.at[0], (twin, z))
    extra = remote(grad_out.at[mine], grad_twin.at[mine], core_sem.at[1], core_recv.at[1], (twin, z))
    extra_in = remote(grad_out.at[other], grad_twin.at[other], core_sem.at[1], core_recv.at[1], (twin, z))
    swap.start()

    @pl.when(core == 1)
    def _():
        extra.start()

    swap_in.wait_recv()

    @pl.loop(0, half_heads)
    def _(j):
        h = core * half_heads + j
        pair[j] = (after[h] + grad_twin[h].astype(F32)).astype(BF16)

    def pair_copy(d):
        return remote(pair, pair_in.at[d - 1], pair_sem.at[d - 1], pair_recv.at[d - 1],
                      ((me + n_ctx - 2 * d) % n_ctx, z))

    for d in range(1, n_chips):
        @pl.when(chip >= d)
        def _():
            pair_copy(d).start()

    @pl.loop(0, heads)
    def _(h):
        attend(blocks - 1, h)

    query_out = pltpu.make_async_copy(qo_buf, qo_hbm, out_sem.at[2 * blocks])
    query_out.start()

    for d in range(1, n_chips):
        @pl.when(chip + d < n_chips)
        def _():
            pair_copy(d).wait_recv()

        @pl.when(chip + d >= n_chips)
        def _():
            pair_in[d - 1] = jnp.zeros(pair_in.shape[1:], BF16)

    @pl.loop(0, half_heads)
    def _(j):
        total = pair_in[0, j].astype(F32)
        for d in range(2, n_chips):
            total = total + pair_in[d - 1, j].astype(F32)
        rest[j] = total

    last = remote(rest, rest_in, core_sem.at[2], core_recv.at[2], (twin, z))
    last.start()

    @pl.when(core == 0)
    def _():
        extra_in.wait_recv()

    last.wait_recv()

    @pl.loop(0, half_heads)
    def _(j):
        after[core * half_heads + j] = rest[j]
        after[(1 - core) * half_heads + j] = rest_in[j]

    @pl.when(core == 0)
    def _():
        @pl.loop(0, heads)
        def _(h):
            after[h] = after[h] + grad_twin[h].astype(F32)

    outs = []
    for c in reversed(range(blocks)):
        at = pl.ds(c * block, block)

        @pl.loop(0, heads)
        def _(h):
            state = after[h]
            low_state = state.astype(BF16)
            key = key_part[at, head(h)] + mm(v_buf[at, head(h)], low_state, NT)
            value = value_part[at, head(h)] + mm(k_buf[at, head(h)], low_state, NN)
            ko_buf[at, head(h)] = (factor * key).astype(BF16)
            vo_buf[at, head(h)] = (factor * value).astype(BF16)
            after[h] = state + grad_sums[c, h]

        outs.append(pltpu.make_async_copy(ko_buf.at[at, :], ko_hbm.at[at, :], out_sem.at[c]))
        outs.append(pltpu.make_async_copy(vo_buf.at[at, :], vo_hbm.at[at, :], out_sem.at[blocks + c]))
        outs[-2].start()
        outs[-1].start()

    swap.wait_send()
    last.wait_send()

    @pl.when(core == 1)
    def _():
        extra.wait_send()

    for d in range(1, n_ctx):
        @pl.when(me + d < n_ctx)
        def _():
            remote(kv_out, kv_in.at[d - 1], kv_sem.at[d - 1], kv_recv.at[d - 1], (twin, z)).wait_send()

    for d in range(1, n_chips):
        @pl.when(chip >= d)
        def _():
            pair_copy(d).wait_send()

    @pl.when(is_end)
    def _():
        for p in range(pieces):
            far_send(p).wait_send()

        @pl.loop(0, chunks)
        def _(i):
            lg_from_hbm(i, ends_sem, mid).wait_send()

    @pl.when(is_mid)
    def _():
        for p in range(pieces):
            far_share(p).wait_send()

        @pl.loop(0, chunks)
        def _(i):
            lg_from_hbm(i, ends_sem, end).wait_send()
            lg_from_hbm(i, mids_sem, mid2).wait_send()
            lg_forward(i).wait_send()
            part_send(i).wait_send()

    query_out.wait()
    for out in outs:
        out.wait()


def fused(q, k, v, lg, w, n_ctx, factor):
    tokens, width = lg.shape
    columns = w.shape[0]
    heads = columns // HEAD
    chunks = 8
    blocks = 4
    pieces = 4
    dma = pltpu.SemaphoreType.DMA
    vmem = pltpu.VMEM
    state = (heads, HEAD, HEAD)
    half = (heads // 2, HEAD, HEAD)
    whole = (tokens, columns)
    chips = n_ctx // 2
    any_spec = pl.BlockSpec(memory_space=pl.ANY)
    return pl.pallas_call(
        functools.partial(gather_kernel, n_ctx, factor),
        out_shape=[jax.ShapeDtypeStruct(whole, BF16)] * 3,
        in_specs=[any_spec] * 5,
        out_specs=[any_spec] * 3,
        scratch_shapes=[
            vmem(whole, BF16), vmem(whole, BF16), vmem(whole, BF16), vmem(whole, BF16),
            vmem((tokens, 4 * width), BF16), vmem(w.shape, BF16), vmem((columns, 2 * width), BF16),
            vmem(whole, BF16), vmem(whole, BF16),
            vmem(whole, BF16), vmem(whole, BF16), vmem(whole, BF16), vmem(whole, F32), vmem(whole, F32),
            vmem((blocks,) + state, F32), vmem((blocks,) + state, BF16), vmem((blocks,) + state, F32), vmem(state, F32),
            vmem(state, BF16), vmem((n_ctx - 1,) + state, BF16), vmem(state, BF16), vmem(state, BF16),
            vmem(half, BF16), vmem((chips - 1,) + half, BF16), vmem(half, F32), vmem(half, F32),
            dma((5,)), dma((chunks,)), dma((chunks,)), dma((4, chunks)), dma((chunks,)),
            dma((chunks,)), dma((chunks,)),
            dma((pieces,)), dma((pieces,)), dma((pieces,)), dma((pieces,)),
            dma((n_ctx - 1,)), dma((n_ctx - 1,)), dma((chips - 1,)), dma((chips - 1,)),
            dma((3,)), dma((3,)), dma((2 * blocks + 1,)),
        ],
        compiler_params=pltpu.CompilerParams(
            collective_id=0, has_side_effects=True, vmem_limit_bytes=62 * 1024 * 1024),
    )(q, k, v, lg, w)


def gather_plain(q, k, v, lg, w):
    tokens, columns = q.shape
    heads = columns // HEAD
    me = lax.axis_index("ctx")
    g = lax.dot_general(lax.all_gather(lg, "tp", axis=1, tiled=True), w, NT, preferred_element_type=F32).astype(BF16)
    three = (tokens, heads, HEAD)
    kv_here = jnp.einsum("lbg,lbz->bgz", k.reshape(three), v.reshape(three), preferred_element_type=F32)
    grad_here = jnp.einsum("lbg,lbz->bgz", q.reshape(three), g.reshape(three), preferred_element_type=F32)

    def pick(mine, lower):
        stacked = lax.all_gather(mine[None], "ctx", axis=0, tiled=True)
        index = jnp.arange(stacked.shape[0])
        chosen = index < me if lower else index > me
        return jnp.sum(jnp.where(chosen[:, None, None, None], stacked, 0.0), 0).astype(BF16)

    return g, pick(kv_here, True), pick(grad_here, False)


def local(q, k, v, lg, w):
    n_ctx = lax.axis_size("ctx")
    n_tp = lax.axis_size("tp")
    factor = float((HEAD * q.shape[0] * n_ctx) ** (-0.5))
    if n_tp == 4 and n_ctx % 2 == 0 and n_ctx > 2 and q.shape[0] % 1024 == 0 and q.shape[1] % 256 == 0:
        return tuple(fused(q, k, v, lg, w, n_ctx, factor))
    g, kv_before, grad_after = gather_plain(q, k, v, lg, w)
    return tuple(attention(q, k, v, g, kv_before, grad_after, factor))


def solution(mesh):
    return jax.shard_map(
        local,
        mesh=mesh,
        in_specs=(P("ctx", "tp"), P("ctx", "tp"), P("ctx", "tp"), P("ctx", "tp"), P("tp", None)),
        out_specs=(P("ctx", "tp"), P("ctx", "tp"), P("ctx", "tp")),
        check_vma=False,
    )
```

```python
import functools

import jax
import jax.numpy as jnp
from jax import lax
from jax.experimental import pallas as pl
from jax.experimental.pallas import tpu as pltpu
from jax.sharding import PartitionSpec as P

HEAD = 128
MESH = pl.DeviceIdType.MESH
F32 = jnp.float32
BF16 = jnp.bfloat16
NT = (((1,), (1,)), ((), ()))
NN = (((1,), (0,)), ((), ()))
TN = (((0,), (0,)), ((), ()))


def mm(a, b, dims):
    return lax.dot_general(a, b, dims, preferred_element_type=F32)


def attention_head(read, state_kv, state_grad, write, tokens, size, factor):
    count = tokens // size
    pieces = [read(i) for i in range(count)]
    rows = lax.broadcasted_iota(jnp.int32, (size, size), 0)
    cols = lax.broadcasted_iota(jnp.int32, (size, size), 1)
    causal = rows >= cols
    after = [None] * count
    total = state_grad
    for i in reversed(range(count)):
        after[i] = total.astype(BF16)
        if i:
            q, _, _, g = pieces[i]
            total = total + mm(q, g, TN)
    before = state_kv
    for i in range(count):
        q, k, v, g = pieces[i]
        inner_grad = jnp.where(causal, mm(g, v, NT), 0.0).astype(BF16)
        inner_query = jnp.where(causal, mm(q, k, NT), 0.0).astype(BF16)
        query = mm(inner_grad, k, NN) + mm(g, before.astype(BF16), NT)
        key = mm(inner_grad, q, TN) + mm(v, after[i], NT)
        value = mm(inner_query, g, TN) + mm(k, after[i], NN)
        write(i, (factor * query).astype(BF16), (factor * key).astype(BF16), (factor * value).astype(BF16))
        if i < count - 1:
            before = before + mm(k, v, TN)


def attention_kernel(size, factor, q_ref, k_ref, v_ref, g_ref, kv_ref, grad_ref, qo_ref, ko_ref, vo_ref):
    tokens = q_ref.shape[0]

    def read(i):
        at = pl.ds(i * size, size)
        return q_ref[at, :], k_ref[at, :], v_ref[at, :], g_ref[at, :]

    def write(i, query, key, value):
        at = pl.ds(i * size, size)
        qo_ref[at, :] = query
        ko_ref[at, :] = key
        vo_ref[at, :] = value

    attention_head(read, kv_ref[0].astype(F32), grad_ref[0].astype(F32), write, tokens, size, factor)


def attention(q, k, v, g, kv_before, grad_after, factor):
    tokens, columns = q.shape
    size = min(256, tokens)
    rows = pl.BlockSpec((tokens, HEAD), lambda h: (0, h))
    state = pl.BlockSpec((1, HEAD, HEAD), lambda h: (h, 0, 0))
    return pl.pallas_call(
        functools.partial(attention_kernel, size, factor),
        grid=(columns // HEAD,),
        out_shape=[jax.ShapeDtypeStruct(q.shape, BF16)] * 3,
        in_specs=[rows] * 4 + [state] * 2,
        out_specs=[rows] * 3,
    )(q, k, v, g, kv_before, grad_after)


def gather_kernel(
    n_ctx, factor, q_hbm, k_hbm, v_hbm, lg_hbm, w_hbm, qo_hbm, ko_hbm, vo_hbm,
    q_buf, k_buf, v_buf, g_ref, lg, w, far, part_out, part_in,
    qo_buf, ko_buf, vo_buf, key_part, value_part, kv_sums, kv_state, grad_sums, after,
    kv_out, kv_in, grad_out, grad_twin, pair, pair_in, rest, rest_in,
    load_sem, ends_sem, mids_sem, lg_recv, fwd_sem, part_sem, part_recv,
    far_sem, far_recv, twin_sem, twin_recv, kv_sem, kv_recv, pair_sem, pair_recv, core_sem, core_recv, out_sem,
):
    me = lax.axis_index("ctx")
    z = lax.axis_index("tp")
    tokens, width = lg_hbm.shape
    columns = w_hbm.shape[0]
    heads = columns // HEAD
    chunks = lg_recv.shape[1]
    size = tokens // chunks
    pieces = far_sem.shape[0]
    half = columns // 2
    piece = half // pieces
    twin = me + 1 - 2 * (me % 2)
    core = me % 2
    is_end = (z == 0) | (z == 3)
    is_mid = (z == 1) | (z == 2)
    low = z // 2
    end = 3 * low
    mid = 1 + low
    mid2 = 2 - low
    end2 = 3 - end
    far_col = pl.multiple_of((1 - low) * 2 * width, 2 * width)
    near_col = pl.multiple_of(low * 2 * width, 2 * width)

    def col(part):
        return pl.ds(pl.multiple_of(part * width, width), width)

    def row(i):
        return pl.ds(pl.multiple_of(i * size, size), size)

    barrier = pltpu.get_barrier_semaphore()
    for d in range(1, n_ctx):
        pl.semaphore_signal(barrier, inc=1, device_id=((me + d) % n_ctx, z), device_id_type=MESH)

    @pl.when(is_end)
    def _():
        pl.semaphore_signal(barrier, inc=1, device_id=(me, mid), device_id_type=MESH)
        pl.semaphore_wait(barrier, n_ctx)

    @pl.when(is_mid)
    def _():
        pl.semaphore_signal(barrier, inc=1, device_id=(me, end), device_id_type=MESH)
        pl.semaphore_signal(barrier, inc=1, device_id=(me, mid2), device_id_type=MESH)
        pl.semaphore_wait(barrier, n_ctx + 1)

    def remote(src, dst, send, recv, target):
        return pltpu.make_async_remote_copy(
            src_ref=src, dst_ref=dst, send_sem=send, recv_sem=recv, device_id=target, device_id_type=MESH)

    def lg_from_hbm(i, sems, target_z):
        return remote(lg_hbm.at[row(i), :], lg.at[row(i), col(z)], sems.at[i], lg_recv.at[z, i], (me, target_z))

    def lg_forward(i):
        place = lg.at[row(i), col(end)]
        return remote(place, place, fwd_sem.at[i], lg_recv.at[end, i], (me, mid2))

    def lg_arrival(part, i):
        place = lg.at[row(i), col(part)]
        return remote(place, place, fwd_sem.at[i], lg_recv.at[part, i], (me, mid2))

    def far_rows(which, p):
        return pl.ds(pl.multiple_of(which * half + p * piece, piece), piece)

    def far_send(p):
        return remote(w_hbm.at[far_rows(core, p), pl.ds(far_col, 2 * width)], far.at[far_rows(core, p), :],
                      far_sem.at[p], far_recv.at[p], (me, mid))

    def far_share(p):
        place = far.at[far_rows(core, p), :]
        return remote(place, place, twin_sem.at[p], twin_recv.at[p], (twin, z))

    def far_twin(p):
        place = far.at[far_rows(1 - core, p), :]
        return remote(place, place, twin_sem.at[p], twin_recv.at[p], (twin, z))

    def part_send(i):
        return remote(part_out.at[row(i), :], part_in.at[row(i), :], part_sem.at[i], part_recv.at[i], (me, end))

    @pl.when(is_end)
    def _():
        for p in range(pieces):
            far_send(p).start()

        @pl.loop(0, chunks)
        def _(i):
            lg_from_hbm(i, ends_sem, mid).start()

    @pl.when(is_mid)
    def _():
        @pl.loop(0, chunks)
        def _(i):
            lg_from_hbm(i, ends_sem, end).start()
            lg_from_hbm(i, mids_sem, mid2).start()

    loads = [
        pltpu.make_async_copy(k_hbm, k_buf, load_sem.at[0]),
        pltpu.make_async_copy(v_hbm, v_buf, load_sem.at[1]),
        pltpu.make_async_copy(q_hbm, q_buf, load_sem.at[2]),
        pltpu.make_async_copy(lg_hbm, lg.at[:, col(z)], load_sem.at[3]),
        pltpu.make_async_copy(w_hbm, w, load_sem.at[4]),
    ]
    for load in loads:
        load.start()
    loads[0].wait()
    loads[1].wait()

    def head(h):
        return pl.ds(pl.multiple_of(h * HEAD, HEAD), HEAD)

    blocks = kv_sums.shape[0]
    block = tokens // blocks
    per = chunks // blocks
    half_heads = heads // 2
    rows_at = lax.broadcasted_iota(jnp.int32, (block, block), 0)
    cols_at = lax.broadcasted_iota(jnp.int32, (block, block), 1)
    causal = rows_at >= cols_at

    def span(c):
        return pl.ds(pl.multiple_of(c * block, block), block)

    @pl.loop(0, heads)
    def _(h):
        total = jnp.zeros((HEAD, HEAD), F32)
        for c in range(blocks):
            here = mm(k_buf[span(c), head(h)], v_buf[span(c), head(h)], TN)
            kv_sums[c, h] = here
            total = total + here
        kv_out[h] = total.astype(BF16)

    for d in range(1, n_ctx):
        @pl.when(me + d < n_ctx)
        def _():
            remote(kv_out, kv_in.at[d - 1], kv_sem.at[d - 1], kv_recv.at[d - 1], ((me + d) % n_ctx, z)).start()
    for load in loads[2:]:
        load.wait()

    tile = min(256, columns)

    def finish_kv():
        for d in range(1, n_ctx):
            @pl.when(me >= d)
            def _():
                remote(kv_in.at[d - 1], kv_in.at[d - 1], kv_sem.at[d - 1], kv_recv.at[d - 1], (twin, z)).wait_recv()

            @pl.when(me < d)
            def _():
                kv_in[d - 1] = jnp.zeros(kv_in.shape[1:], BF16)

        @pl.loop(0, heads)
        def _(h):
            total = kv_in[0, h].astype(F32)
            for d in range(2, n_ctx):
                total = total + kv_in[d - 1, h].astype(F32)
            for c in range(blocks):
                kv_state[c, h] = total.astype(BF16)
                total = total + kv_sums[c, h]

    def attend(c, h):
        at, hd = span(c), head(h)
        q, k, v, g = q_buf[at, hd], k_buf[at, hd], v_buf[at, hd], g_ref[at, hd]
        inner_grad = jnp.where(causal, mm(g, v, NT), 0.0).astype(BF16)
        inner_query = jnp.where(causal, mm(q, k, NT), 0.0).astype(BF16)
        query = mm(inner_grad, k, NN) + mm(g, kv_state[c, h], NT)
        qo_buf[at, hd] = (factor * query).astype(BF16)
        key_part[at, hd] = mm(inner_grad, q, TN)
        value_part[at, hd] = mm(inner_query, g, TN)

    def attend_step(i):
        @pl.when(i >= per)
        def _():
            share = heads // per

            @pl.loop(0, share)
            def _(j):
                attend(i // per - 1, (i % per) * share + j)

    def sum_step(i):
        @pl.when(i % per == per - 1)
        def _():
            @pl.loop(0, heads)
            def _(h):
                c = i // per
                grad_sums[c, h] = mm(q_buf[span(c), head(h)], g_ref[span(c), head(h)], TN)

    def project(left, right, out_ref, at):
        @pl.loop(0, columns // tile)
        def _(n):
            out = pl.ds(pl.multiple_of(n * tile, tile), tile)
            out_ref[at, out] = mm(left[at, :], right[out, :], NT)

    near = pl.ds(near_col, 2 * width)
    middle = pl.ds(width, 2 * width)
    far_mid2 = pl.ds(pl.multiple_of(low * width, width), width)
    far_end2 = pl.ds(pl.multiple_of((1 - low) * width, width), width)

    @pl.when(is_end)
    def _():
        @pl.loop(0, blocks)
        def _(c):
            for j in range(per):
                lg_arrival(mid, c * per + j).wait_recv()
            project(lg.at[:, near], w.at[:, near], key_part, span(c))

        finish_kv()

        @pl.loop(0, chunks)
        def _(i):
            attend_step(i)
            part_send(i).wait_recv()
            g_ref[row(i), :] = (key_part[row(i), :] + part_in[row(i), :].astype(F32)).astype(BF16)
            sum_step(i)

    @pl.when(is_mid)
    def _():
        for c in range(blocks):
            for j in range(per):
                lg_arrival(mid2, c * per + j).wait_recv()
            far_send(c).wait_recv()
            far_share(c).start()
            project(lg.at[:, middle], w.at[:, middle], key_part, span(c))
        lg_arrival(end, 0).wait_recv()
        lg_forward(0).start()
        finish_kv()
        for p in range(pieces):
            far_twin(p).wait_recv()

        @pl.loop(0, blocks)
        def _(c):
            project(lg.at[:, col(mid2)], far.at[:, far_mid2], value_part, span(c))

        @pl.loop(0, chunks)
        def _(i):
            @pl.when(i < chunks - 1)
            def _():
                lg_arrival(end, i + 1).wait_recv()
                lg_forward(i + 1).start()

            attend_step(i)
            lg_arrival(end2, i).wait_recv()

            @pl.loop(0, columns // tile)
            def _(n):
                out = pl.ds(pl.multiple_of(n * tile, tile), tile)
                total = value_part[row(i), out] + mm(lg[row(i), col(end2)], far[out, far_end2], NT)
                part_out[row(i), out] = total.astype(BF16)

            part_send(i).start()

            @pl.loop(0, columns // tile)
            def _(n):
                out = pl.ds(pl.multiple_of(n * tile, tile), tile)
                total = key_part[row(i), out] + mm(lg[row(i), col(end)], w[out, col(end)], NT)
                g_ref[row(i), out] = (total + mm(lg[row(i), col(end2)], w[out, col(end2)], NT)).astype(BF16)

            sum_step(i)

    chip = me // 2
    n_chips = n_ctx // 2
    mine = pl.ds(pl.multiple_of(core * half_heads, half_heads), half_heads)
    other = pl.ds(pl.multiple_of((1 - core) * half_heads, half_heads), half_heads)

    @pl.loop(0, heads)
    def _(h):
        total = grad_sums[0, h]
        for c in range(1, blocks):
            total = total + grad_sums[c, h]
        after[h] = total
        grad_out[h] = total.astype(BF16)

    swap = remote(grad_out.at[other], grad_twin.at[other], core_sem.at[0], core_recv.at[0], (twin, z))
    swap_in = remote(grad_out.at[mine], grad_twin.at[mine], core_sem.at[0], core_recv.at[0], (twin, z))
    extra = remote(grad_out.at[mine], grad_twin.at[mine], core_sem.at[1], core_recv.at[1], (twin, z))
    extra_in = remote(grad_out.at[other], grad_twin.at[other], core_sem.at[1], core_recv.at[1], (twin, z))
    swap.start()

    @pl.when(core == 1)
    def _():
        extra.start()

    swap_in.wait_recv()

    @pl.loop(0, half_heads)
    def _(j):
        h = core * half_heads + j
        pair[j] = (after[h] + grad_twin[h].astype(F32)).astype(BF16)

    def pair_copy(d):
        return remote(pair, pair_in.at[d - 1], pair_sem.at[d - 1], pair_recv.at[d - 1],
                      ((me + n_ctx - 2 * d) % n_ctx, z))

    for d in range(1, n_chips):
        @pl.when(chip >= d)
        def _():
            pair_copy(d).start()

    @pl.loop(0, heads)
    def _(h):
        attend(blocks - 1, h)

    query_out = pltpu.make_async_copy(qo_buf, qo_hbm, out_sem.at[2 * blocks])
    query_out.start()

    for d in range(1, n_chips):
        @pl.when(chip + d < n_chips)
        def _():
            pair_copy(d).wait_recv()

        @pl.when(chip + d >= n_chips)
        def _():
            pair_in[d - 1] = jnp.zeros(pair_in.shape[1:], BF16)

    @pl.loop(0, half_heads)
    def _(j):
        total = pair_in[0, j].astype(F32)
        for d in range(2, n_chips):
            total = total + pair_in[d - 1, j].astype(F32)
        rest[j] = total

    last = remote(rest, rest_in, core_sem.at[2], core_recv.at[2], (twin, z))
    last.start()

    @pl.when(core == 0)
    def _():
        extra_in.wait_recv()

    last.wait_recv()

    @pl.loop(0, half_heads)
    def _(j):
        after[core * half_heads + j] = rest[j]
        after[(1 - core) * half_heads + j] = rest_in[j]

    @pl.when(core == 0)
    def _():
        @pl.loop(0, heads)
        def _(h):
            after[h] = after[h] + grad_twin[h].astype(F32)

    outs = []
    for c in reversed(range(blocks)):
        at = pl.ds(c * block, block)

        @pl.loop(0, heads)
        def _(h):
            state = after[h]
            low_state = state.astype(BF16)
            key = key_part[at, head(h)] + mm(v_buf[at, head(h)], low_state, NT)
            value = value_part[at, head(h)] + mm(k_buf[at, head(h)], low_state, NN)
            ko_buf[at, head(h)] = (factor * key).astype(BF16)
            vo_buf[at, head(h)] = (factor * value).astype(BF16)
            after[h] = state + grad_sums[c, h]

        outs.append(pltpu.make_async_copy(ko_buf.at[at, :], ko_hbm.at[at, :], out_sem.at[c]))
        outs.append(pltpu.make_async_copy(vo_buf.at[at, :], vo_hbm.at[at, :], out_sem.at[blocks + c]))
        outs[-2].start()
        outs[-1].start()

    swap.wait_send()
    last.wait_send()

    @pl.when(core == 1)
    def _():
        extra.wait_send()

    for d in range(1, n_ctx):
        @pl.when(me + d < n_ctx)
        def _():
            remote(kv_out, kv_in.at[d - 1], kv_sem.at[d - 1], kv_recv.at[d - 1], (twin, z)).wait_send()

    for d in range(1, n_chips):
        @pl.when(chip >= d)
        def _():
            pair_copy(d).wait_send()

    @pl.when(is_end)
    def _():
        for p in range(pieces):
            far_send(p).wait_send()

        @pl.loop(0, chunks)
        def _(i):
            lg_from_hbm(i, ends_sem, mid).wait_send()

    @pl.when(is_mid)
    def _():
        for p in range(pieces):
            far_share(p).wait_send()

        @pl.loop(0, chunks)
        def _(i):
            lg_from_hbm(i, ends_sem, end).wait_send()
            lg_from_hbm(i, mids_sem, mid2).wait_send()
            lg_forward(i).wait_send()
            part_send(i).wait_send()

    query_out.wait()
    for out in outs:
        out.wait()


def fused(q, k, v, lg, w, n_ctx, factor):
    tokens, width = lg.shape
    columns = w.shape[0]
    heads = columns // HEAD
    chunks = 8
    blocks = 4
    pieces = 4
    dma = pltpu.SemaphoreType.DMA
    vmem = pltpu.VMEM
    state = (heads, HEAD, HEAD)
    half = (heads // 2, HEAD, HEAD)
    whole = (tokens, columns)
    chips = n_ctx // 2
    any_spec = pl.BlockSpec(memory_space=pl.ANY)
    return pl.pallas_call(
        functools.partial(gather_kernel, n_ctx, factor),
        out_shape=[jax.ShapeDtypeStruct(whole, BF16)] * 3,
        in_specs=[any_spec] * 5,
        out_specs=[any_spec] * 3,
        scratch_shapes=[
            vmem(whole, BF16), vmem(whole, BF16), vmem(whole, BF16), vmem(whole, BF16),
            vmem((tokens, 4 * width), BF16), vmem(w.shape, BF16), vmem((columns, 2 * width), BF16),
            vmem(whole, BF16), vmem(whole, BF16),
            vmem(whole, BF16), vmem(whole, BF16), vmem(whole, BF16), vmem(whole, F32), vmem(whole, F32),
            vmem((blocks,) + state, F32), vmem((blocks,) + state, BF16), vmem((blocks,) + state, F32), vmem(state, F32),
            vmem(state, BF16), vmem((n_ctx - 1,) + state, BF16), vmem(state, BF16), vmem(state, BF16),
            vmem(half, BF16), vmem((chips - 1,) + half, BF16), vmem(half, F32), vmem(half, F32),
            dma((5,)), dma((chunks,)), dma((chunks,)), dma((4, chunks)), dma((chunks,)),
            dma((chunks,)), dma((chunks,)),
            dma((pieces,)), dma((pieces,)), dma((pieces,)), dma((pieces,)),
            dma((n_ctx - 1,)), dma((n_ctx - 1,)), dma((chips - 1,)), dma((chips - 1,)),
            dma((3,)), dma((3,)), dma((2 * blocks + 1,)),
        ],
        compiler_params=pltpu.CompilerParams(
            collective_id=0, has_side_effects=True, vmem_limit_bytes=62 * 1024 * 1024),
    )(q, k, v, lg, w)


def gather_plain(q, k, v, lg, w):
    tokens, columns = q.shape
    heads = columns // HEAD
    me = lax.axis_index("ctx")
    g = lax.dot_general(lax.all_gather(lg, "tp", axis=1, tiled=True), w, NT, preferred_element_type=F32).astype(BF16)
    three = (tokens, heads, HEAD)
    kv_here = jnp.einsum("lbg,lbz->bgz", k.reshape(three), v.reshape(three), preferred_element_type=F32)
    grad_here = jnp.einsum("lbg,lbz->bgz", q.reshape(three), g.reshape(three), preferred_element_type=F32)

    def pick(mine, lower):
        stacked = lax.all_gather(mine[None], "ctx", axis=0, tiled=True)
        index = jnp.arange(stacked.shape[0])
        chosen = index < me if lower else index > me
        return jnp.sum(jnp.where(chosen[:, None, None, None], stacked, 0.0), 0).astype(BF16)

    return g, pick(kv_here, True), pick(grad_here, False)


def local(q, k, v, lg, w):
    n_ctx = lax.axis_size("ctx")
    n_tp = lax.axis_size("tp")
    factor = float((HEAD * q.shape[0] * n_ctx) ** (-0.5))
    if n_tp == 4 and n_ctx % 2 == 0 and n_ctx > 2 and q.shape[0] % 1024 == 0 and q.shape[1] % 256 == 0:
        return tuple(fused(q, k, v, lg, w, n_ctx, factor))
    g, kv_before, grad_after = gather_plain(q, k, v, lg, w)
    return tuple(attention(q, k, v, g, kv_before, grad_after, factor))


def solution(mesh):
    return jax.shard_map(
        local,
        mesh=mesh,
        in_specs=(P("ctx", "tp"), P("ctx", "tp"), P("ctx", "tp"), P("ctx", "tp"), P("tp", None)),
        out_specs=(P("ctx", "tp"), P("ctx", "tp"), P("ctx", "tp")),
        check_vma=False,
    )
```

```python
import functools

import jax
import jax.numpy as jnp
from jax import lax
from jax.experimental import pallas as pl
from jax.experimental.pallas import tpu as pltpu
from jax.sharding import PartitionSpec as P

HEAD = 128
MESH = pl.DeviceIdType.MESH
F32 = jnp.float32
BF16 = jnp.bfloat16
NT = (((1,), (1,)), ((), ()))
NN = (((1,), (0,)), ((), ()))
TN = (((0,), (0,)), ((), ()))


def mm(a, b, dims):
    return lax.dot_general(a, b, dims, preferred_element_type=F32)


def attention_head(read, state_kv, state_grad, write, tokens, size, factor):
    count = tokens // size
    pieces = [read(i) for i in range(count)]
    rows = lax.broadcasted_iota(jnp.int32, (size, size), 0)
    cols = lax.broadcasted_iota(jnp.int32, (size, size), 1)
    causal = rows >= cols
    after = [None] * count
    total = state_grad
    for i in reversed(range(count)):
        after[i] = total.astype(BF16)
        if i:
            q, _, _, g = pieces[i]
            total = total + mm(q, g, TN)
    before = state_kv
    for i in range(count):
        q, k, v, g = pieces[i]
        inner_grad = jnp.where(causal, mm(g, v, NT), 0.0).astype(BF16)
        inner_query = jnp.where(causal, mm(q, k, NT), 0.0).astype(BF16)
        query = mm(inner_grad, k, NN) + mm(g, before.astype(BF16), NT)
        key = mm(inner_grad, q, TN) + mm(v, after[i], NT)
        value = mm(inner_query, g, TN) + mm(k, after[i], NN)
        write(i, (factor * query).astype(BF16), (factor * key).astype(BF16), (factor * value).astype(BF16))
        if i < count - 1:
            before = before + mm(k, v, TN)


def attention_kernel(size, factor, q_ref, k_ref, v_ref, g_ref, kv_ref, grad_ref, qo_ref, ko_ref, vo_ref):
    tokens = q_ref.shape[0]

    def read(i):
        at = pl.ds(i * size, size)
        return q_ref[at, :], k_ref[at, :], v_ref[at, :], g_ref[at, :]

    def write(i, query, key, value):
        at = pl.ds(i * size, size)
        qo_ref[at, :] = query
        ko_ref[at, :] = key
        vo_ref[at, :] = value

    attention_head(read, kv_ref[0].astype(F32), grad_ref[0].astype(F32), write, tokens, size, factor)


def attention(q, k, v, g, kv_before, grad_after, factor):
    tokens, columns = q.shape
    size = min(256, tokens)
    rows = pl.BlockSpec((tokens, HEAD), lambda h: (0, h))
    state = pl.BlockSpec((1, HEAD, HEAD), lambda h: (h, 0, 0))
    return pl.pallas_call(
        functools.partial(attention_kernel, size, factor),
        grid=(columns // HEAD,),
        out_shape=[jax.ShapeDtypeStruct(q.shape, BF16)] * 3,
        in_specs=[rows] * 4 + [state] * 2,
        out_specs=[rows] * 3,
    )(q, k, v, g, kv_before, grad_after)


def gather_kernel(
    n_ctx, factor, q_hbm, k_hbm, v_hbm, lg_hbm, w_hbm, qo_buf, ko_buf, vo_buf,
    q_buf, k_buf, v_buf, g_ref, lg, w, far, part_out, part_in,
    key_part, value_part, kv_sums, kv_state, grad_sums, after,
    kv_out, kv_in, grad_out, grad_twin, pair, pair_in, rest, rest_in,
    load_sem, ends_sem, mids_sem, lg_recv, fwd_sem, part_sem, part_recv,
    far_sem, far_recv, twin_sem, twin_recv, kv_sem, kv_recv, pair_sem, pair_recv, core_sem, core_recv,
):
    me = lax.axis_index("ctx")
    z = lax.axis_index("tp")
    tokens, width = lg_hbm.shape
    columns = w_hbm.shape[0]
    heads = columns // HEAD
    chunks = lg_recv.shape[1]
    size = tokens // chunks
    pieces = far_sem.shape[0]
    quarter = columns // 4
    piece = quarter // pieces
    share = me % 4
    twin = me + 1 - 2 * (me % 2)
    core = me % 2
    pal = me + 2 - 4 * ((me // 2) % 2)
    pal_share = (share + 2) % 4
    is_end = (z == 0) | (z == 3)
    is_mid = (z == 1) | (z == 2)
    low = z // 2
    end = 3 * low
    mid = 1 + low
    mid2 = 2 - low
    end2 = 3 - end
    far_col = pl.multiple_of((1 - low) * 2 * width, 2 * width)
    near_col = pl.multiple_of(low * 2 * width, 2 * width)

    def col(part):
        return pl.ds(pl.multiple_of(part * width, width), width)

    def row(i):
        return pl.ds(pl.multiple_of(i * size, size), size)

    barrier = pltpu.get_barrier_semaphore()
    for d in range(1, n_ctx):
        pl.semaphore_signal(barrier, inc=1, device_id=((me + d) % n_ctx, z), device_id_type=MESH)

    @pl.when(is_end)
    def _():
        pl.semaphore_signal(barrier, inc=1, device_id=(me, mid), device_id_type=MESH)
        pl.semaphore_wait(barrier, n_ctx)

    @pl.when(is_mid)
    def _():
        pl.semaphore_signal(barrier, inc=1, device_id=(me, end), device_id_type=MESH)
        pl.semaphore_signal(barrier, inc=1, device_id=(me, mid2), device_id_type=MESH)
        pl.semaphore_wait(barrier, n_ctx + 1)

    def remote(src, dst, send, recv, target):
        return pltpu.make_async_remote_copy(
            src_ref=src, dst_ref=dst, send_sem=send, recv_sem=recv, device_id=target, device_id_type=MESH)

    def lg_from_hbm(i, sems, target_z):
        return remote(lg_hbm.at[row(i), :], lg.at[row(i), col(z)], sems.at[i], lg_recv.at[z, i], (me, target_z))

    def lg_forward(i):
        place = lg.at[row(i), col(end)]
        return remote(place, place, fwd_sem.at[i], lg_recv.at[end, i], (me, mid2))

    def lg_arrival(part, i):
        place = lg.at[row(i), col(part)]
        return remote(place, place, fwd_sem.at[i], lg_recv.at[part, i], (me, mid2))

    def far_rows(which, p):
        return pl.ds(pl.multiple_of(which * quarter + p * piece, piece), piece)

    def far_send(p):
        return remote(w_hbm.at[far_rows(share, p), pl.ds(far_col, 2 * width)], far.at[far_rows(share, p), :],
                      far_sem.at[p], far_recv.at[p], (me, mid))

    def far_share(which, p, slot, target):
        place = far.at[far_rows(which, p), :]
        return remote(place, place, twin_sem.at[slot, p], twin_recv.at[slot, p], (target, z))

    def part_send(i):
        return remote(part_out.at[row(i), :], part_in.at[row(i), :], part_sem.at[i], part_recv.at[i], (me, end))

    @pl.when(is_end)
    def _():
        for p in range(pieces):
            far_send(p).start()

        @pl.loop(0, chunks)
        def _(i):
            lg_from_hbm(i, ends_sem, mid).start()

    @pl.when(is_mid)
    def _():
        @pl.loop(0, chunks)
        def _(i):
            lg_from_hbm(i, ends_sem, end).start()
            lg_from_hbm(i, mids_sem, mid2).start()

    loads = [
        pltpu.make_async_copy(k_hbm, k_buf, load_sem.at[0]),
        pltpu.make_async_copy(v_hbm, v_buf, load_sem.at[1]),
        pltpu.make_async_copy(q_hbm, q_buf, load_sem.at[2]),
        pltpu.make_async_copy(lg_hbm, lg.at[:, col(z)], load_sem.at[3]),
        pltpu.make_async_copy(w_hbm, w, load_sem.at[4]),
    ]
    for load in loads:
        load.start()
    loads[0].wait()
    loads[1].wait()

    def head(h):
        return pl.ds(pl.multiple_of(h * HEAD, HEAD), HEAD)

    blocks = kv_sums.shape[0]
    block = tokens // blocks
    per = chunks // blocks
    ahead = 3
    half_heads = heads // 2
    rows_at = lax.broadcasted_iota(jnp.int32, (block, block), 0)
    cols_at = lax.broadcasted_iota(jnp.int32, (block, block), 1)
    causal = rows_at >= cols_at

    def span(c):
        return pl.ds(pl.multiple_of(c * block, block), block)

    @pl.loop(0, heads)
    def _(h):
        total = jnp.zeros((HEAD, HEAD), F32)
        for c in range(blocks):
            here = mm(k_buf[span(c), head(h)], v_buf[span(c), head(h)], TN)
            kv_sums[c, h] = here
            total = total + here
        kv_out[h] = total.astype(BF16)

    for d in range(1, n_ctx):
        @pl.when(me + d < n_ctx)
        def _():
            remote(kv_out, kv_in.at[d - 1], kv_sem.at[d - 1], kv_recv.at[d - 1], ((me + d) % n_ctx, z)).start()
    for load in loads[2:]:
        load.wait()

    tile = min(256, columns)

    def finish_kv():
        for d in range(1, n_ctx):
            @pl.when(me >= d)
            def _():
                remote(kv_in.at[d - 1], kv_in.at[d - 1], kv_sem.at[d - 1], kv_recv.at[d - 1], (twin, z)).wait_recv()

            @pl.when(me < d)
            def _():
                kv_in[d - 1] = jnp.zeros(kv_in.shape[1:], BF16)

        @pl.loop(0, heads)
        def _(h):
            total = kv_in[0, h].astype(F32)
            for d in range(2, n_ctx):
                total = total + kv_in[d - 1, h].astype(F32)
            for c in range(blocks):
                kv_state[c, h] = total.astype(BF16)
                total = total + kv_sums[c, h]

    def attend(c, h):
        at, hd = span(c), head(h)
        q, k, v, g = q_buf[at, hd], k_buf[at, hd], v_buf[at, hd], g_ref[at, hd]
        inner_grad = jnp.where(causal, mm(g, v, NT), 0.0).astype(BF16)
        inner_query = jnp.where(causal, mm(q, k, NT), 0.0).astype(BF16)
        query = mm(inner_grad, k, NN) + mm(g, kv_state[c, h], NT)
        qo_buf[at, hd] = (factor * query).astype(BF16)
        key_part[at, hd] = mm(inner_grad, q, TN)
        value_part[at, hd] = mm(inner_query, g, TN)

    def attend_step(i):
        @pl.when(i >= per)
        def _():
            share = heads // per

            @pl.loop(0, share)
            def _(j):
                attend(i // per - 1, (i % per) * share + j)

    def sum_step(i):
        @pl.when(i % per == per - 1)
        def _():
            @pl.loop(0, heads)
            def _(h):
                c = i // per
                grad_sums[c, h] = mm(q_buf[span(c), head(h)], g_ref[span(c), head(h)], TN)

    def project(left, right, out_ref, at):
        @pl.loop(0, columns // tile)
        def _(n):
            out = pl.ds(pl.multiple_of(n * tile, tile), tile)
            out_ref[at, out] = mm(left[at, :], right[out, :], NT)

    near = pl.ds(near_col, 2 * width)
    middle = pl.ds(width, 2 * width)
    far_mid2 = pl.ds(pl.multiple_of(low * width, width), width)
    far_end2 = pl.ds(pl.multiple_of((1 - low) * width, width), width)

    @pl.when(is_end)
    def _():
        @pl.loop(0, blocks)
        def _(c):
            for j in range(per):
                lg_arrival(mid, c * per + j).wait_recv()
            project(lg.at[:, near], w.at[:, near], key_part, span(c))

        finish_kv()

        @pl.loop(0, chunks)
        def _(i):
            attend_step(i)
            part_send(i).wait_recv()
            g_ref[row(i), :] = (key_part[row(i), :] + part_in[row(i), :].astype(F32)).astype(BF16)
            sum_step(i)

    @pl.when(is_mid)
    def _():
        for c in range(blocks):
            for j in range(per):
                lg_arrival(mid2, c * per + j).wait_recv()
            if c < pieces:
                far_send(c).wait_recv()
                far_share(share, c, 0, pal).start()
                far_share(share, c, 1, twin).start()
            if c == pieces:
                for p in range(pieces):
                    far_share(pal_share, p, 0, pal).wait_recv()
                    far_share(pal_share, p, 2, twin).start()
            for i in {2: (0,), 3: (1, 2)}.get(c, ()):
                lg_arrival(end, i).wait_recv()
                lg_forward(i).start()
            project(lg.at[:, middle], w.at[:, middle], key_part, span(c))
        finish_kv()
        for p in range(pieces):
            far_share(share + 1 - 2 * core, p, 1, twin).wait_recv()
            far_share(pal_share + 1 - 2 * core, p, 2, twin).wait_recv()

        @pl.loop(0, blocks)
        def _(c):
            project(lg.at[:, col(mid2)], far.at[:, far_mid2], value_part, span(c))

        @pl.loop(0, chunks)
        def _(i):
            @pl.when(i < chunks - ahead)
            def _():
                lg_arrival(end, i + ahead).wait_recv()
                lg_forward(i + ahead).start()

            attend_step(i)
            lg_arrival(end2, i).wait_recv()

            @pl.loop(0, columns // tile)
            def _(n):
                out = pl.ds(pl.multiple_of(n * tile, tile), tile)
                total = value_part[row(i), out] + mm(lg[row(i), col(end2)], far[out, far_end2], NT)
                part_out[row(i), out] = total.astype(BF16)

            part_send(i).start()

            @pl.loop(0, columns // tile)
            def _(n):
                out = pl.ds(pl.multiple_of(n * tile, tile), tile)
                total = key_part[row(i), out] + mm(lg[row(i), col(end)], w[out, col(end)], NT)
                g_ref[row(i), out] = (total + mm(lg[row(i), col(end2)], w[out, col(end2)], NT)).astype(BF16)

            sum_step(i)

    chip = me // 2
    n_chips = n_ctx // 2
    mine = pl.ds(pl.multiple_of(core * half_heads, half_heads), half_heads)
    other = pl.ds(pl.multiple_of((1 - core) * half_heads, half_heads), half_heads)

    @pl.loop(0, heads)
    def _(h):
        total = grad_sums[0, h]
        for c in range(1, blocks):
            total = total + grad_sums[c, h]
        after[h] = total
        grad_out[h] = total.astype(BF16)

    swap = remote(grad_out.at[other], grad_twin.at[other], core_sem.at[0], core_recv.at[0], (twin, z))
    swap_in = remote(grad_out.at[mine], grad_twin.at[mine], core_sem.at[0], core_recv.at[0], (twin, z))
    extra = remote(grad_out.at[mine], grad_twin.at[mine], core_sem.at[1], core_recv.at[1], (twin, z))
    extra_in = remote(grad_out.at[other], grad_twin.at[other], core_sem.at[1], core_recv.at[1], (twin, z))
    swap.start()

    @pl.when(core == 1)
    def _():
        extra.start()

    swap_in.wait_recv()

    @pl.loop(0, half_heads)
    def _(j):
        h = core * half_heads + j
        pair[j] = (after[h] + grad_twin[h].astype(F32)).astype(BF16)

    def pair_copy(d):
        return remote(pair, pair_in.at[d - 1], pair_sem.at[d - 1], pair_recv.at[d - 1],
                      ((me + n_ctx - 2 * d) % n_ctx, z))

    for d in range(1, n_chips):
        @pl.when(chip >= d)
        def _():
            pair_copy(d).start()

    @pl.loop(0, heads)
    def _(h):
        attend(blocks - 1, h)

    for d in range(1, n_chips):
        @pl.when(chip + d < n_chips)
        def _():
            pair_copy(d).wait_recv()

        @pl.when(chip + d >= n_chips)
        def _():
            pair_in[d - 1] = jnp.zeros(pair_in.shape[1:], BF16)

    @pl.loop(0, half_heads)
    def _(j):
        total = pair_in[0, j].astype(F32)
        for d in range(2, n_chips):
            total = total + pair_in[d - 1, j].astype(F32)
        rest[j] = total

    last = remote(rest, rest_in, core_sem.at[2], core_recv.at[2], (twin, z))
    last.start()

    @pl.when(core == 0)
    def _():
        extra_in.wait_recv()

    last.wait_recv()

    @pl.loop(0, half_heads)
    def _(j):
        after[core * half_heads + j] = rest[j]
        after[(1 - core) * half_heads + j] = rest_in[j]

    @pl.when(core == 0)
    def _():
        @pl.loop(0, heads)
        def _(h):
            after[h] = after[h] + grad_twin[h].astype(F32)

    for c in reversed(range(blocks)):
        at = pl.ds(c * block, block)

        @pl.loop(0, heads)
        def _(h):
            state = after[h]
            low_state = state.astype(BF16)
            key = key_part[at, head(h)] + mm(v_buf[at, head(h)], low_state, NT)
            value = value_part[at, head(h)] + mm(k_buf[at, head(h)], low_state, NN)
            ko_buf[at, head(h)] = (factor * key).astype(BF16)
            vo_buf[at, head(h)] = (factor * value).astype(BF16)
            after[h] = state + grad_sums[c, h]

    swap.wait_send()
    last.wait_send()

    @pl.when(core == 1)
    def _():
        extra.wait_send()

    for d in range(1, n_ctx):
        @pl.when(me + d < n_ctx)
        def _():
            remote(kv_out, kv_in.at[d - 1], kv_sem.at[d - 1], kv_recv.at[d - 1], (twin, z)).wait_send()

    for d in range(1, n_chips):
        @pl.when(chip >= d)
        def _():
            pair_copy(d).wait_send()

    @pl.when(is_end)
    def _():
        for p in range(pieces):
            far_send(p).wait_send()

        @pl.loop(0, chunks)
        def _(i):
            lg_from_hbm(i, ends_sem, mid).wait_send()

    @pl.when(is_mid)
    def _():
        for p in range(pieces):
            far_share(share, p, 0, pal).wait_send()
            far_share(share, p, 1, twin).wait_send()
            far_share(pal_share, p, 2, twin).wait_send()

        @pl.loop(0, chunks)
        def _(i):
            lg_from_hbm(i, ends_sem, end).wait_send()
            lg_from_hbm(i, mids_sem, mid2).wait_send()
            lg_forward(i).wait_send()
            part_send(i).wait_send()


def fused(q, k, v, lg, w, n_ctx, factor):
    tokens, width = lg.shape
    columns = w.shape[0]
    heads = columns // HEAD
    chunks = 8
    blocks = 4
    pieces = 2
    dma = pltpu.SemaphoreType.DMA
    vmem = pltpu.VMEM
    state = (heads, HEAD, HEAD)
    half = (heads // 2, HEAD, HEAD)
    whole = (tokens, columns)
    chips = n_ctx // 2
    any_spec = pl.BlockSpec(memory_space=pl.ANY)
    return pl.pallas_call(
        functools.partial(gather_kernel, n_ctx, factor),
        out_shape=[pltpu.VMEM(whole, BF16)] * 3,
        in_specs=[any_spec] * 5,
        out_specs=[pl.BlockSpec(memory_space=pltpu.VMEM)] * 3,
        scratch_shapes=[
            vmem(whole, BF16), vmem(whole, BF16), vmem(whole, BF16), vmem(whole, BF16),
            vmem((tokens, 4 * width), BF16), vmem(w.shape, BF16), vmem((columns, 2 * width), BF16),
            vmem(whole, BF16), vmem(whole, BF16),
            vmem(whole, F32), vmem(whole, F32),
            vmem((blocks,) + state, F32), vmem((blocks,) + state, BF16), vmem((blocks,) + state, F32), vmem(state, F32),
            vmem(state, BF16), vmem((n_ctx - 1,) + state, BF16), vmem(state, BF16), vmem(state, BF16),
            vmem(half, BF16), vmem((chips - 1,) + half, BF16), vmem(half, F32), vmem(half, F32),
            dma((5,)), dma((chunks,)), dma((chunks,)), dma((4, chunks)), dma((chunks,)),
            dma((chunks,)), dma((chunks,)),
            dma((pieces,)), dma((pieces,)), dma((3, pieces)), dma((3, pieces)),
            dma((n_ctx - 1,)), dma((n_ctx - 1,)), dma((chips - 1,)), dma((chips - 1,)),
            dma((3,)), dma((3,)),
        ],
        compiler_params=pltpu.CompilerParams(
            collective_id=0, has_side_effects=True, vmem_limit_bytes=54 * 1024 * 1024),
    )(q, k, v, lg, w)


def gather_plain(q, k, v, lg, w):
    tokens, columns = q.shape
    heads = columns // HEAD
    me = lax.axis_index("ctx")
    g = lax.dot_general(lax.all_gather(lg, "tp", axis=1, tiled=True), w, NT, preferred_element_type=F32).astype(BF16)
    three = (tokens, heads, HEAD)
    kv_here = jnp.einsum("lbg,lbz->bgz", k.reshape(three), v.reshape(three), preferred_element_type=F32)
    grad_here = jnp.einsum("lbg,lbz->bgz", q.reshape(three), g.reshape(three), preferred_element_type=F32)

    def pick(mine, lower):
        stacked = lax.all_gather(mine[None], "ctx", axis=0, tiled=True)
        index = jnp.arange(stacked.shape[0])
        chosen = index < me if lower else index > me
        return jnp.sum(jnp.where(chosen[:, None, None, None], stacked, 0.0), 0).astype(BF16)

    return g, pick(kv_here, True), pick(grad_here, False)


def local(q, k, v, lg, w):
    n_ctx = lax.axis_size("ctx")
    n_tp = lax.axis_size("tp")
    factor = float((HEAD * q.shape[0] * n_ctx) ** (-0.5))
    if n_tp == 4 and n_ctx % 4 == 0 and q.shape[0] % 1024 == 0 and q.shape[1] % 256 == 0:
        return tuple(fused(q, k, v, lg, w, n_ctx, factor))
    g, kv_before, grad_after = gather_plain(q, k, v, lg, w)
    return tuple(attention(q, k, v, g, kv_before, grad_after, factor))


def solution(mesh):
    return jax.shard_map(
        local,
        mesh=mesh,
        in_specs=(P("ctx", "tp"), P("ctx", "tp"), P("ctx", "tp"), P("ctx", "tp"), P("tp", None)),
        out_specs=(P("ctx", "tp"), P("ctx", "tp"), P("ctx", "tp")),
        check_vma=False,
    )
```

```python
import functools

import jax
import jax.numpy as jnp
from jax import lax
from jax.experimental import pallas as pl
from jax.experimental.pallas import tpu as pltpu
from jax.sharding import PartitionSpec as P

HEAD = 128
MESH = pl.DeviceIdType.MESH
F32 = jnp.float32
BF16 = jnp.bfloat16
NT = (((1,), (1,)), ((), ()))
NN = (((1,), (0,)), ((), ()))
TN = (((0,), (0,)), ((), ()))


def mm(a, b, dims):
    return lax.dot_general(a, b, dims, preferred_element_type=F32)


def attention_head(read, state_kv, state_grad, write, tokens, size, factor):
    count = tokens // size
    pieces = [read(i) for i in range(count)]
    rows = lax.broadcasted_iota(jnp.int32, (size, size), 0)
    cols = lax.broadcasted_iota(jnp.int32, (size, size), 1)
    causal = rows >= cols
    after = [None] * count
    total = state_grad
    for i in reversed(range(count)):
        after[i] = total.astype(BF16)
        if i:
            q, _, _, g = pieces[i]
            total = total + mm(q, g, TN)
    before = state_kv
    for i in range(count):
        q, k, v, g = pieces[i]
        inner_grad = jnp.where(causal, mm(g, v, NT), 0.0).astype(BF16)
        inner_query = jnp.where(causal, mm(q, k, NT), 0.0).astype(BF16)
        query = mm(inner_grad, k, NN) + mm(g, before.astype(BF16), NT)
        key = mm(inner_grad, q, TN) + mm(v, after[i], NT)
        value = mm(inner_query, g, TN) + mm(k, after[i], NN)
        write(i, (factor * query).astype(BF16), (factor * key).astype(BF16), (factor * value).astype(BF16))
        if i < count - 1:
            before = before + mm(k, v, TN)


def attention_kernel(size, factor, q_ref, k_ref, v_ref, g_ref, kv_ref, grad_ref, qo_ref, ko_ref, vo_ref):
    tokens = q_ref.shape[0]

    def read(i):
        at = pl.ds(i * size, size)
        return q_ref[at, :], k_ref[at, :], v_ref[at, :], g_ref[at, :]

    def write(i, query, key, value):
        at = pl.ds(i * size, size)
        qo_ref[at, :] = query
        ko_ref[at, :] = key
        vo_ref[at, :] = value

    attention_head(read, kv_ref[0].astype(F32), grad_ref[0].astype(F32), write, tokens, size, factor)


def attention(q, k, v, g, kv_before, grad_after, factor):
    tokens, columns = q.shape
    size = min(256, tokens)
    rows = pl.BlockSpec((tokens, HEAD), lambda h: (0, h))
    state = pl.BlockSpec((1, HEAD, HEAD), lambda h: (h, 0, 0))
    return pl.pallas_call(
        functools.partial(attention_kernel, size, factor),
        grid=(columns // HEAD,),
        out_shape=[jax.ShapeDtypeStruct(q.shape, BF16)] * 3,
        in_specs=[rows] * 4 + [state] * 2,
        out_specs=[rows] * 3,
    )(q, k, v, g, kv_before, grad_after)


def gather_kernel(
    n_ctx, factor, q_hbm, k_hbm, v_hbm, lg_hbm, w_hbm, qo_buf, ko_buf, vo_buf,
    q_buf, k_buf, v_buf, g_ref, lg, w, far, part_out, part_in,
    key_part, value_part, kv_sums, kv_state, grad_sums, after,
    kv_out, kv_in, grad_out, grad_twin, pair, pair_in, rest, rest_in,
    load_sem, ends_sem, mids_sem, lg_recv, fwd_sem, part_sem, part_recv,
    far_sem, far_recv, twin_sem, twin_recv, kv_sem, kv_recv, pair_sem, pair_recv, core_sem, core_recv,
):
    me = lax.axis_index("ctx")
    z = lax.axis_index("tp")
    tokens, width = lg_hbm.shape
    columns = w_hbm.shape[0]
    heads = columns // HEAD
    chunks = lg_recv.shape[1]
    size = tokens // chunks
    pieces = far_sem.shape[0]
    quarter = columns // 4
    piece = quarter // pieces
    share = me % 4
    twin = me + 1 - 2 * (me % 2)
    core = me % 2
    pal = me + 2 - 4 * ((me // 2) % 2)
    pal_share = (share + 2) % 4
    is_end = (z == 0) | (z == 3)
    is_mid = (z == 1) | (z == 2)
    low = z // 2
    end = 3 * low
    mid = 1 + low
    mid2 = 2 - low
    end2 = 3 - end
    far_col = pl.multiple_of((1 - low) * 2 * width, 2 * width)
    near_col = pl.multiple_of(low * 2 * width, 2 * width)

    def col(part):
        return pl.ds(pl.multiple_of(part * width, width), width)

    def row(i):
        return pl.ds(pl.multiple_of(i * size, size), size)

    barrier = pltpu.get_barrier_semaphore()
    for d in range(1, n_ctx):
        pl.semaphore_signal(barrier, inc=1, device_id=((me + d) % n_ctx, z), device_id_type=MESH)

    @pl.when(is_end)
    def _():
        pl.semaphore_signal(barrier, inc=1, device_id=(me, mid), device_id_type=MESH)
        pl.semaphore_wait(barrier, n_ctx)

    @pl.when(is_mid)
    def _():
        pl.semaphore_signal(barrier, inc=1, device_id=(me, end), device_id_type=MESH)
        pl.semaphore_signal(barrier, inc=1, device_id=(me, mid2), device_id_type=MESH)
        pl.semaphore_wait(barrier, n_ctx + 1)

    def remote(src, dst, send, recv, target):
        return pltpu.make_async_remote_copy(
            src_ref=src, dst_ref=dst, send_sem=send, recv_sem=recv, device_id=target, device_id_type=MESH)

    def lg_from_hbm(i, sems, target_z):
        return remote(lg_hbm.at[row(i), :], lg.at[row(i), col(z)], sems.at[i], lg_recv.at[z, i], (me, target_z))

    def lg_forward(i):
        place = lg.at[row(i), col(end)]
        return remote(place, place, fwd_sem.at[i], lg_recv.at[end, i], (me, mid2))

    def lg_arrival(part, i):
        place = lg.at[row(i), col(part)]
        return remote(place, place, fwd_sem.at[i], lg_recv.at[part, i], (me, mid2))

    def far_rows(which, p):
        return pl.ds(pl.multiple_of(which * quarter + p * piece, piece), piece)

    def far_send(p):
        return remote(w_hbm.at[far_rows(share, p), pl.ds(far_col, 2 * width)], far.at[far_rows(share, p), :],
                      far_sem.at[p], far_recv.at[p], (me, mid))

    def far_share(which, p, slot, target):
        place = far.at[far_rows(which, p), :]
        return remote(place, place, twin_sem.at[slot, p], twin_recv.at[slot, p], (target, z))

    def part_send(i):
        return remote(part_out.at[row(i), :], part_in.at[row(i), :], part_sem.at[i], part_recv.at[i], (me, end))

    @pl.when(is_end)
    def _():
        for p in range(pieces):
            far_send(p).start()

        @pl.loop(0, chunks)
        def _(i):
            lg_from_hbm(i, ends_sem, mid).start()

    @pl.when(is_mid)
    def _():
        @pl.loop(0, chunks)
        def _(i):
            lg_from_hbm(i, ends_sem, end).start()
            lg_from_hbm(i, mids_sem, mid2).start()

    loads = [
        pltpu.make_async_copy(k_hbm, k_buf, load_sem.at[0]),
        pltpu.make_async_copy(v_hbm, v_buf, load_sem.at[1]),
        pltpu.make_async_copy(q_hbm, q_buf, load_sem.at[2]),
        pltpu.make_async_copy(lg_hbm, lg.at[:, col(z)], load_sem.at[3]),
        pltpu.make_async_copy(w_hbm, w, load_sem.at[4]),
    ]
    for load in loads:
        load.start()
    loads[0].wait()
    loads[1].wait()

    def head(h):
        return pl.ds(pl.multiple_of(h * HEAD, HEAD), HEAD)

    blocks = kv_sums.shape[0]
    block = tokens // blocks
    per = chunks // blocks
    ahead = 3 * chunks // 8
    half_heads = heads // 2
    rows_at = lax.broadcasted_iota(jnp.int32, (block, block), 0)
    cols_at = lax.broadcasted_iota(jnp.int32, (block, block), 1)
    causal = rows_at >= cols_at

    def span(c):
        return pl.ds(pl.multiple_of(c * block, block), block)

    @pl.loop(0, heads)
    def _(h):
        total = jnp.zeros((HEAD, HEAD), F32)
        for c in range(blocks):
            here = mm(k_buf[span(c), head(h)], v_buf[span(c), head(h)], TN)
            kv_sums[c, h] = here
            total = total + here
        kv_out[h] = total.astype(BF16)

    for d in range(1, n_ctx):
        @pl.when(me + d < n_ctx)
        def _():
            remote(kv_out, kv_in.at[d - 1], kv_sem.at[d - 1], kv_recv.at[d - 1], ((me + d) % n_ctx, z)).start()
    for load in loads[2:]:
        load.wait()

    tile = min(512, columns)

    def finish_kv():
        for d in range(1, n_ctx):
            @pl.when(me >= d)
            def _():
                remote(kv_in.at[d - 1], kv_in.at[d - 1], kv_sem.at[d - 1], kv_recv.at[d - 1], (twin, z)).wait_recv()

            @pl.when(me < d)
            def _():
                kv_in[d - 1] = jnp.zeros(kv_in.shape[1:], BF16)

        @pl.loop(0, heads)
        def _(h):
            total = kv_in[0, h].astype(F32)
            for d in range(2, n_ctx):
                total = total + kv_in[d - 1, h].astype(F32)
            for c in range(blocks):
                kv_state[c, h] = total.astype(BF16)
                total = total + kv_sums[c, h]

    def attend(c, h):
        at, hd = span(c), head(h)
        q, k, v, g = q_buf[at, hd], k_buf[at, hd], v_buf[at, hd], g_ref[at, hd]
        inner_grad = jnp.where(causal, mm(g, v, NT), 0.0).astype(BF16)
        inner_query = jnp.where(causal, mm(q, k, NT), 0.0).astype(BF16)
        query = mm(inner_grad, k, NN) + mm(g, kv_state[c, h], NT)
        qo_buf[at, hd] = (factor * query).astype(BF16)
        key_part[at, hd] = mm(inner_grad, q, TN)
        value_part[at, hd] = mm(inner_query, g, TN)

    def attend_step(i):
        @pl.when(i >= per)
        def _():
            share = heads // per

            @pl.loop(0, share)
            def _(j):
                attend(i // per - 1, (i % per) * share + j)

    def sum_step(i):
        @pl.when(i % per == per - 1)
        def _():
            @pl.loop(0, heads)
            def _(h):
                c = i // per
                grad_sums[c, h] = mm(q_buf[span(c), head(h)], g_ref[span(c), head(h)], TN)

    def project(left, right, out_ref, at):
        @pl.loop(0, columns // tile)
        def _(n):
            out = pl.ds(pl.multiple_of(n * tile, tile), tile)
            out_ref[at, out] = mm(left[at, :], right[out, :], NT)

    near = pl.ds(near_col, 2 * width)
    middle = pl.ds(width, 2 * width)
    far_mid2 = pl.ds(pl.multiple_of(low * width, width), width)
    far_end2 = pl.ds(pl.multiple_of((1 - low) * width, width), width)

    @pl.when(is_end)
    def _():
        @pl.loop(0, blocks)
        def _(c):
            for j in range(per):
                lg_arrival(mid, c * per + j).wait_recv()
            project(lg.at[:, near], w.at[:, near], key_part, span(c))

        finish_kv()

        @pl.loop(0, chunks)
        def _(i):
            attend_step(i)
            part_send(i).wait_recv()
            g_ref[row(i), :] = (key_part[row(i), :] + part_in[row(i), :].astype(F32)).astype(BF16)
            sum_step(i)

    @pl.when(is_mid)
    def _():
        for c in range(blocks):
            for j in range(per):
                lg_arrival(mid2, c * per + j).wait_recv()
            if c < pieces:
                far_send(c).wait_recv()
                far_share(share, c, 0, pal).start()
                far_share(share, c, 1, twin).start()
            if c == pieces:
                for p in range(pieces):
                    far_share(pal_share, p, 0, pal).wait_recv()
                    far_share(pal_share, p, 2, twin).start()
            for i in {2: range(ahead // 3), 3: range(ahead // 3, ahead)}.get(c, ()):
                lg_arrival(end, i).wait_recv()
                lg_forward(i).start()
            project(lg.at[:, middle], w.at[:, middle], key_part, span(c))
        finish_kv()
        for p in range(pieces):
            far_share(share + 1 - 2 * core, p, 1, twin).wait_recv()
            far_share(pal_share + 1 - 2 * core, p, 2, twin).wait_recv()

        @pl.loop(0, blocks)
        def _(c):
            project(lg.at[:, col(mid2)], far.at[:, far_mid2], value_part, span(c))

        @pl.loop(0, chunks)
        def _(i):
            @pl.when(i < chunks - ahead)
            def _():
                lg_arrival(end, i + ahead).wait_recv()
                lg_forward(i + ahead).start()

            attend_step(i)
            lg_arrival(end2, i).wait_recv()

            @pl.loop(0, columns // tile)
            def _(n):
                out = pl.ds(pl.multiple_of(n * tile, tile), tile)
                total = value_part[row(i), out] + mm(lg[row(i), col(end2)], far[out, far_end2], NT)
                part_out[row(i), out] = total.astype(BF16)

            part_send(i).start()

            @pl.when(i % 2 == 1)
            def _():
                both = pl.ds(pl.multiple_of((i // 2) * 2 * size, 2 * size), 2 * size)

                @pl.loop(0, columns // tile)
                def _(n):
                    out = pl.ds(pl.multiple_of(n * tile, tile), tile)
                    total = key_part[both, out] + mm(lg[both, col(end)], w[out, col(end)], NT)
                    g_ref[both, out] = (total + mm(lg[both, col(end2)], w[out, col(end2)], NT)).astype(BF16)

            sum_step(i)

    chip = me // 2
    n_chips = n_ctx // 2
    mine = pl.ds(pl.multiple_of(core * half_heads, half_heads), half_heads)
    other = pl.ds(pl.multiple_of((1 - core) * half_heads, half_heads), half_heads)

    @pl.loop(0, heads)
    def _(h):
        total = grad_sums[0, h]
        for c in range(1, blocks):
            total = total + grad_sums[c, h]
        after[h] = total
        grad_out[h] = total.astype(BF16)

    swap = remote(grad_out.at[other], grad_twin.at[other], core_sem.at[0], core_recv.at[0], (twin, z))
    swap_in = remote(grad_out.at[mine], grad_twin.at[mine], core_sem.at[0], core_recv.at[0], (twin, z))
    extra = remote(grad_out.at[mine], grad_twin.at[mine], core_sem.at[1], core_recv.at[1], (twin, z))
    extra_in = remote(grad_out.at[other], grad_twin.at[other], core_sem.at[1], core_recv.at[1], (twin, z))
    swap.start()

    @pl.when(core == 1)
    def _():
        extra.start()

    swap_in.wait_recv()

    @pl.loop(0, half_heads)
    def _(j):
        h = core * half_heads + j
        pair[j] = (after[h] + grad_twin[h].astype(F32)).astype(BF16)

    def pair_copy(d):
        return remote(pair, pair_in.at[d - 1], pair_sem.at[d - 1], pair_recv.at[d - 1],
                      ((me + n_ctx - 2 * d) % n_ctx, z))

    for d in range(1, n_chips):
        @pl.when(chip >= d)
        def _():
            pair_copy(d).start()

    @pl.loop(0, heads)
    def _(h):
        attend(blocks - 1, h)

    for d in range(1, n_chips):
        @pl.when(chip + d < n_chips)
        def _():
            pair_copy(d).wait_recv()

        @pl.when(chip + d >= n_chips)
        def _():
            pair_in[d - 1] = jnp.zeros(pair_in.shape[1:], BF16)

    @pl.loop(0, half_heads)
    def _(j):
        total = pair_in[0, j].astype(F32)
        for d in range(2, n_chips):
            total = total + pair_in[d - 1, j].astype(F32)
        rest[j] = total

    last = remote(rest, rest_in, core_sem.at[2], core_recv.at[2], (twin, z))
    last.start()

    @pl.when(core == 0)
    def _():
        extra_in.wait_recv()

    last.wait_recv()

    @pl.loop(0, half_heads)
    def _(j):
        after[core * half_heads + j] = rest[j]
        after[(1 - core) * half_heads + j] = rest_in[j]

    @pl.when(core == 0)
    def _():
        @pl.loop(0, heads)
        def _(h):
            after[h] = after[h] + grad_twin[h].astype(F32)

    for c in reversed(range(blocks)):
        at = pl.ds(c * block, block)

        @pl.loop(0, heads)
        def _(h):
            state = after[h]
            low_state = state.astype(BF16)
            key = key_part[at, head(h)] + mm(v_buf[at, head(h)], low_state, NT)
            value = value_part[at, head(h)] + mm(k_buf[at, head(h)], low_state, NN)
            ko_buf[at, head(h)] = (factor * key).astype(BF16)
            vo_buf[at, head(h)] = (factor * value).astype(BF16)
            after[h] = state + grad_sums[c, h]

    swap.wait_send()
    last.wait_send()

    @pl.when(core == 1)
    def _():
        extra.wait_send()

    for d in range(1, n_ctx):
        @pl.when(me + d < n_ctx)
        def _():
            remote(kv_out, kv_in.at[d - 1], kv_sem.at[d - 1], kv_recv.at[d - 1], (twin, z)).wait_send()

    for d in range(1, n_chips):
        @pl.when(chip >= d)
        def _():
            pair_copy(d).wait_send()

    @pl.when(is_end)
    def _():
        for p in range(pieces):
            far_send(p).wait_send()

        @pl.loop(0, chunks)
        def _(i):
            lg_from_hbm(i, ends_sem, mid).wait_send()

    @pl.when(is_mid)
    def _():
        for p in range(pieces):
            far_share(share, p, 0, pal).wait_send()
            far_share(share, p, 1, twin).wait_send()
            far_share(pal_share, p, 2, twin).wait_send()

        @pl.loop(0, chunks)
        def _(i):
            lg_from_hbm(i, ends_sem, end).wait_send()
            lg_from_hbm(i, mids_sem, mid2).wait_send()
            lg_forward(i).wait_send()
            part_send(i).wait_send()


def fused(q, k, v, lg, w, n_ctx, factor):
    tokens, width = lg.shape
    columns = w.shape[0]
    heads = columns // HEAD
    chunks = 8
    blocks = 4
    pieces = 2
    dma = pltpu.SemaphoreType.DMA
    vmem = pltpu.VMEM
    state = (heads, HEAD, HEAD)
    half = (heads // 2, HEAD, HEAD)
    whole = (tokens, columns)
    chips = n_ctx // 2
    any_spec = pl.BlockSpec(memory_space=pl.ANY)
    return pl.pallas_call(
        functools.partial(gather_kernel, n_ctx, factor),
        out_shape=[pltpu.VMEM(whole, BF16)] * 3,
        in_specs=[any_spec] * 5,
        out_specs=[pl.BlockSpec(memory_space=pltpu.VMEM)] * 3,
        scratch_shapes=[
            vmem(whole, BF16), vmem(whole, BF16), vmem(whole, BF16), vmem(whole, BF16),
            vmem((tokens, 4 * width), BF16), vmem(w.shape, BF16), vmem((columns, 2 * width), BF16),
            vmem(whole, BF16), vmem(whole, BF16),
            vmem(whole, F32), vmem(whole, F32),
            vmem((blocks,) + state, F32), vmem((blocks,) + state, BF16), vmem((blocks,) + state, F32), vmem(state, F32),
            vmem(state, BF16), vmem((n_ctx - 1,) + state, BF16), vmem(state, BF16), vmem(state, BF16),
            vmem(half, BF16), vmem((chips - 1,) + half, BF16), vmem(half, F32), vmem(half, F32),
            dma((5,)), dma((chunks,)), dma((chunks,)), dma((4, chunks)), dma((chunks,)),
            dma((chunks,)), dma((chunks,)),
            dma((pieces,)), dma((pieces,)), dma((3, pieces)), dma((3, pieces)),
            dma((n_ctx - 1,)), dma((n_ctx - 1,)), dma((chips - 1,)), dma((chips - 1,)),
            dma((3,)), dma((3,)),
        ],
        compiler_params=pltpu.CompilerParams(
            collective_id=0, has_side_effects=True, vmem_limit_bytes=54 * 1024 * 1024),
    )(q, k, v, lg, w)


def gather_plain(q, k, v, lg, w):
    tokens, columns = q.shape
    heads = columns // HEAD
    me = lax.axis_index("ctx")
    g = lax.dot_general(lax.all_gather(lg, "tp", axis=1, tiled=True), w, NT, preferred_element_type=F32).astype(BF16)
    three = (tokens, heads, HEAD)
    kv_here = jnp.einsum("lbg,lbz->bgz", k.reshape(three), v.reshape(three), preferred_element_type=F32)
    grad_here = jnp.einsum("lbg,lbz->bgz", q.reshape(three), g.reshape(three), preferred_element_type=F32)

    def pick(mine, lower):
        stacked = lax.all_gather(mine[None], "ctx", axis=0, tiled=True)
        index = jnp.arange(stacked.shape[0])
        chosen = index < me if lower else index > me
        return jnp.sum(jnp.where(chosen[:, None, None, None], stacked, 0.0), 0).astype(BF16)

    return g, pick(kv_here, True), pick(grad_here, False)


def local(q, k, v, lg, w):
    n_ctx = lax.axis_size("ctx")
    n_tp = lax.axis_size("tp")
    factor = float((HEAD * q.shape[0] * n_ctx) ** (-0.5))
    if n_tp == 4 and n_ctx % 4 == 0 and q.shape[0] % 1024 == 0 and q.shape[1] % 256 == 0:
        return tuple(fused(q, k, v, lg, w, n_ctx, factor))
    g, kv_before, grad_after = gather_plain(q, k, v, lg, w)
    return tuple(attention(q, k, v, g, kv_before, grad_after, factor))


def solution(mesh):
    return jax.shard_map(
        local,
        mesh=mesh,
        in_specs=(P("ctx", "tp"), P("ctx", "tp"), P("ctx", "tp"), P("ctx", "tp"), P("tp", None)),
        out_specs=(P("ctx", "tp"), P("ctx", "tp"), P("ctx", "tp")),
        check_vma=False,
    )
```
